256 devices in a mesh: section: 16 (over x, z_lo), replica: 16 (over y, z_hi, core).
Axes of the slice: x: 4, y: 4, z: 8 (z_hi: 2, z_lo: 4; z = z_hi * 4 + z_lo), core: 2. Of those that a mesh axis runs over, the one named last changes fastest.
Arguments:
- wa_local: bfloat16 [16, 16, 576, 1536], P('section', 'replica'), may hold values from -0.25 to 0.25
- wb_local: bfloat16 [16, 16, 1536, 576], P('section', 'replica'), may hold values from -0.15625 to 0.15625
- wa_master: float32 [16, 576, 1536], P('section', 'replica'), may hold values from -0.25 to 0.25
- wb_master: float32 [16, 1536, 576], P('section', None, 'replica'), may hold values from -0.15625 to 0.15625
- wa_moment: float32 [16, 576, 1536], P('section', 'replica'), may hold values from -0.075 to 0.075
- wb_moment: float32 [16, 1536, 576], P('section', None, 'replica'), may hold values from -0.045927934 to 0.045927934
- counts: int32 [16], P('section'), may hold values from 1 to 6
- inputs: bfloat16 [4096, 576], P('replica'), may hold values from -6 to 6
Outputs:
- wa_next: float32 [16, 576, 1536], P('section', 'replica')
- wb_next: float32 [16, 1536, 576], P('section', None, 'replica')
- boundary: bfloat16 [16, 4096, 576], P('section', 'replica')
The draws below stay inside these ranges and needn't reach their ends.
Inputs may be any that keep to these rules, and one draw needn't show every extreme that they name: `counts`: each section applies its layer at least once and at most 6 times.
All inputs are finite; a program needn't handle non-finite values.
Results may differ from the reference program's by a relative error of at most 0.03.
Values may be sent and summed in bfloat16 or wider, within the bound.
No kernel may reach another device: no remote copies, remote signals or barrier semaphores. Data moves between devices by JAX's collectives and lax.ppermute only.
A program may use at most 64 MiB of HBM per device.

```python
import jax
import jax.numpy as jnp
from jax import lax

D = 576
FS = 1536
MOST_LAYERS = 6
TOKENS = 4096
N_SECTION = 16
N_REPLICA = 16


def touch_ends(entries, key, smallest, largest):
    longest = entries.shape.index(max(entries.shape))
    spots = []
    for shift in (0, 1):
        where = [jax.random.randint(jax.random.fold_in(key, axis), (), 0, length) for axis, length in enumerate(entries.shape)]
        where[longest] = (where[longest] + shift) % entries.shape[longest]
        spots.append(tuple(where))
    return entries.at[spots[0]].set(smallest).at[spots[1]].set(largest)


def block_scale(key, dims, cuts, low, largest):
    loudness, own = 1.0, jax.random.fold_in(key, 6)
    for axis_at, blocks in cuts:
        draws = jnp.exp(jax.random.uniform(jax.random.fold_in(own, axis_at), (blocks,), jnp.float32, low / len(cuts), largest / len(cuts)))
        loudness = loudness * jnp.repeat(draws, dims[axis_at] // blocks).reshape([-1 if axis == axis_at else 1 for axis in range(len(dims))])
    return loudness


def gaussian(stream_key, shape, scale, most, shards=(), kind=jnp.bfloat16):
    entries = scale * jax.random.normal(stream_key, shape, jnp.float32)
    if shards:
        entries = entries * block_scale(stream_key, shape, shards, -0.22, 0.18)
    return jnp.clip(entries, -most, most).astype(kind)


def setup_inputs(seed: int = 0) -> dict:
    key_of = jax.random.split(jax.random.key(seed), 9)
    wa_local = gaussian(key_of[0], (N_SECTION, N_REPLICA, D, FS), D ** -0.5, 0.25, ((0, 16), (1, 16)))
    wb_local = gaussian(key_of[1], (N_SECTION, N_REPLICA, FS, D), FS ** -0.5, 0.15625, ((0, 16), (1, 16)))
    wa_master = gaussian(key_of[2], (N_SECTION, D, FS), D ** -0.5, 0.25, ((0, 16), (1, 16)), jnp.float32)
    wb_master = gaussian(key_of[3], (N_SECTION, FS, D), FS ** -0.5, 0.15625, ((0, 16), (2, 16)), jnp.float32)
    wa_moment = gaussian(key_of[4], (N_SECTION, D, FS), (0.3 * D ** -0.5), 0.075, ((0, 16), (1, 16)), jnp.float32)
    wb_moment = gaussian(key_of[5], (N_SECTION, FS, D), (0.3 * FS ** -0.5), 0.045927934, ((0, 16), (2, 16)), jnp.float32)
    counts = touch_ends(jax.random.randint(key_of[6], (N_SECTION,), 1, MOST_LAYERS + 1), jax.random.fold_in(key_of[6], 1), 1, MOST_LAYERS).astype(jnp.int32)
    inputs = gaussian(key_of[7], (TOKENS, D), 1.0, 6.0, ((0, 16),))
    return dict(wa_local=wa_local, wb_local=wb_local, wa_master=wa_master, wb_master=wb_master, wa_moment=wa_moment, wb_moment=wb_moment, counts=counts, inputs=inputs)


def outer_update(master, moment, local):
    summed = lax.optimization_barrier(jnp.sum(local.astype(jnp.float32), axis=0))
    mean_value = summed / N_REPLICA
    delta = master - mean_value
    moment_new = 0.9 * moment + delta
    return master - 0.7 * (delta + 0.9 * moment_new)

def run_section(rows_in, layer_count, wa_bf, wb_bf):

    def apply_layer(step_index, stream):
        square_mean = lax.optimization_barrier(jnp.mean(stream * stream, axis=-1, keepdims=True))
        normed = (stream * lax.rsqrt(square_mean + 1e-05)).astype(jnp.bfloat16)
        gate_value = jnp.dot(normed, wa_bf, preferred_element_type=jnp.float32)
        hidden = jax.nn.silu(gate_value).astype(jnp.bfloat16)
        return stream + jnp.dot(hidden, wb_bf, preferred_element_type=jnp.float32)
    stream = lax.fori_loop(0, layer_count, apply_layer, rows_in.astype(jnp.float32))
    return stream.astype(jnp.bfloat16)

def reference(wa_local, wb_local, wa_master, wb_master, wa_moment, wb_moment, counts, inputs):
    wa_list = []
    wb_list = []
    for section_index in range(N_SECTION):
        wa_list.append(outer_update(wa_master[section_index], wa_moment[section_index], wa_local[section_index]))
        wb_list.append(outer_update(wb_master[section_index], wb_moment[section_index], wb_local[section_index]))
    wa_next = jnp.stack(wa_list)
    wb_next = jnp.stack(wb_list)
    current = inputs
    outputs = []
    for section_index in range(N_SECTION):
        current = run_section(current, counts[section_index], wa_list[section_index].astype(jnp.bfloat16), wb_list[section_index].astype(jnp.bfloat16))
        outputs.append(current)
    return (wa_next, wb_next, jnp.stack(outputs))
```

```python
import functools

import jax
import jax.numpy as jnp
from jax import lax
from jax.experimental import pallas as pl
from jax.experimental.pallas import tpu as pltpu
from jax.sharding import PartitionSpec as P

AXES = ("section", "replica")
F32, BF16 = jnp.float32, jnp.bfloat16
BOTH = (0, 1)
ORDER = (0, -1, 1, 2)
PLACE = (0, 2, 3, 1)


def device(x, y, z, core):
    x, y, z = x % 4, y % 4, z % 8
    return (x * 4 + z % 4) * 16 + y * 4 + (z // 4) * 2 + core


def route(move, cores=BOTH, planes=range(4)):
    return [
        (device(x, y, z, core), device(*move(x, y, z, core)))
        for x in planes
        for y in range(4)
        for z in range(8)
        for core in cores
    ]


def y_step(by, cores=BOTH):
    return route(lambda x, y, z, core: (x, y + by, z, core), cores)


def z_step(by, cores=BOTH):
    return route(lambda x, y, z, core: (x, y, z + by, core), cores)


def core_swap(cores=BOTH):
    return route(lambda x, y, z, core: (x, y, z, 1 - core), cores)


def send(block, pairs):
    return lax.ppermute(block, AXES, pairs)


def outer_update(master, moment, mean_value):
    delta = master - mean_value
    moment_new = 0.9 * moment + delta
    return master - 0.7 * (delta + 0.9 * moment_new)


def relay_kernel(step, has_held, info, rows_ref, *refs):
    refs = list(refs)
    held_ref = refs.pop(0) if has_held else None
    own, crossed = refs[:8], refs[8:16]
    out_ref, last_ref, wa_v, wb_v, stream, sem_a, sem_b = refs[16:]
    x, z_low, y, core = info[0], info[1], info[2], info[3]
    hidden = wa_v.shape[2]
    half = hidden // 2
    quarter = own[0].shape[1]

    def load(section):
        place = info[8 + lax.rem(section - z_low + 4, 4)]

        def copy(src, dst_v, side, sem):
            row = lax.rem(y + ORDER[side] + 4, 4) * quarter
            pltpu.make_async_copy(
                src,
                dst_v.at[section, pl.ds(pl.multiple_of(row, 16), quarter)],
                sem.at[section],
            ).start()

        def fetch(a_bufs, b_bufs):
            for message in range(4):

                @pl.when(place == message)
                def _(message=message):
                    for side in range(4):
                        copy(a_bufs[2 * message + side // 2].at[side % 2], wa_v, side, sem_a)

            for part in range(2):

                @pl.when(place // 2 == part)
                def _(part=part):
                    for side in range(4):
                        copy(b_bufs[2 * side + part].at[lax.rem(place, 2)], wb_v, side, sem_b)

        @pl.when(core == 0)
        def _():
            fetch(own, crossed)

        @pl.when(core == 1)
        def _():
            fetch(crossed, own)

    @pl.when(x == step)
    def _():
        load(0)
        stream[...] = rows_ref[...].astype(F32)

        def run(section, carry):
            @pl.when(section < 3)
            def _():
                load(section + 1)

            pltpu.make_async_copy(wa_v.at[section], wa_v.at[section], sem_a.at[section]).wait()
            pltpu.make_async_copy(wb_v.at[section], wb_v.at[section], sem_b.at[section]).wait()

            def layer(step, carry):
                value = stream[...]
                scale = lax.rsqrt(jnp.mean(value * value, axis=-1, keepdims=True) + 1e-5)
                narrow = value.astype(BF16)
                total = None
                for at in range(2):
                    columns = pl.ds(at * half, half)
                    gate = jnp.dot(narrow, wa_v[section, :, columns], preferred_element_type=F32)
                    gate = gate * (0.5 * scale)
                    act = (gate + gate * jnp.tanh(gate)).astype(BF16)
                    part = lax.dot_general(
                        act,
                        wb_v[section, :, columns],
                        (((1,), (1,)), ((), ())),
                        preferred_element_type=F32,
                    )
                    total = part if total is None else total + part
                stream[...] = value + total
                return carry

            lax.fori_loop(0, info[4 + lax.rem(z_low - section + 4, 4)], layer, 0)
            done = stream[...].astype(BF16)
            out_ref[section] = done
            last_ref[...] = done
            stream[...] = done.astype(F32)
            return carry

        lax.fori_loop(0, 4, run, 0)

    if has_held:

        @pl.when(x != step)
        def _():
            out_ref[...] = held_ref[...]


def relay(step, info, rows, held, own, crossed):
    vmem, hbm = pl.BlockSpec(memory_space=pltpu.VMEM), pl.BlockSpec(memory_space=pltpu.HBM)
    count, width = rows.shape
    height, hidden = 4 * own[0].shape[1], own[0].shape[2]
    helds = [] if held is None else [held]
    return pl.pallas_call(
        functools.partial(relay_kernel, step, held is not None),
        name="relay",
        out_shape=(
            jax.ShapeDtypeStruct((4, count, width), BF16),
            jax.ShapeDtypeStruct((count, width), BF16),
        ),
        in_specs=[pl.BlockSpec(memory_space=pltpu.SMEM), vmem]
        + [vmem] * len(helds)
        + [hbm] * (len(own) + len(crossed)),
        out_specs=(vmem, vmem),
        scratch_shapes=[
            pltpu.VMEM((4, height, hidden), BF16),
            pltpu.VMEM((4, height, hidden), BF16),
            pltpu.VMEM((count, width), F32),
            pltpu.SemaphoreType.DMA((4,)),
            pltpu.SemaphoreType.DMA((4,)),
        ],
        compiler_params=pltpu.CompilerParams(vmem_limit_bytes=56 << 20),
    )(info, rows, *helds, *own, *crossed)


def body(wa_local, wb_local, wa_master, wb_master, wa_moment, wb_moment, counts, inputs):
    section, replica = lax.axis_index("section"), lax.axis_index("replica")
    x, z_low = section // 4, section % 4
    y, z_high, core = replica // 4, (replica // 2) % 2, replica % 2
    first = core == 0
    replicas = lax.axis_size("replica")
    owned, hidden = wa_master.shape[1], wa_master.shape[2]
    chunk = 2 * owned

    a_own, b_own = wa_local[0, 0], wb_local[0, 0].T

    a_got = send(a_own, core_swap((1,)))
    b_got = send(b_own, core_swap((0,)))
    pair_sum = jnp.where(
        first,
        a_own.astype(F32) + a_got.astype(F32),
        b_own.astype(F32) + b_got.astype(F32),
    ).astype(BF16)
    quarters = pair_sum.reshape(4, 2, chunk, hidden)

    def quarter(by):
        return lax.dynamic_index_in_dim(quarters, (y + by) % 4, 0, keepdims=False)

    across, ahead, behind, mine = quarter(2), quarter(1), quarter(3), quarter(0)
    from_behind = send(jnp.stack([across[0], ahead[1]]), y_step(1))
    from_ahead = send(jnp.stack([across[1], behind[0]]), y_step(-1))
    layers = [counts] + [
        send(counts, route(lambda x, y, z, core, by=by: (x, y, z // 4 * 4 + (z + by) % 4, core)))
        for by in (1, 2, 3)
    ]
    info = jnp.concatenate([jnp.stack([x, z_low, y, core]), *layers, jnp.array(PLACE, jnp.int32)])
    from_behind, from_ahead, info = lax.optimization_barrier((from_behind, from_ahead, info))
    top_got = send((ahead[0].astype(F32) + from_behind[0].astype(F32)).astype(BF16), y_step(1))
    bottom_got = send((behind[1].astype(F32) + from_ahead[0].astype(F32)).astype(BF16), y_step(-1))
    top = mine[0].astype(F32) + from_ahead[1].astype(F32) + top_got.astype(F32)
    bottom = mine[1].astype(F32) + from_behind[1].astype(F32) + bottom_got.astype(F32)
    low = z_high == 0
    z_got = send(jnp.where(low, bottom, top).astype(BF16), z_step(4))
    mean_value = (jnp.where(low, top, bottom) + z_got.astype(F32)) / replicas

    a_state = jnp.concatenate([wa_master, wa_moment])
    b_state = jnp.concatenate([wb_master, wb_moment]).transpose(0, 2, 1)
    kept = jnp.where(first, a_state, b_state)
    state_got = send(jnp.where(first, b_state, a_state), core_swap())
    state = jnp.where(
        first,
        jnp.concatenate([kept, state_got], axis=1),
        jnp.concatenate([state_got, kept], axis=1),
    )
    updated = outer_update(state[0], state[1], mean_value)
    ours = jnp.where(first, updated[:owned], updated[owned:])
    theirs = send(jnp.where(first, updated[owned:], updated[:owned]), core_swap())

    def turn(by):
        return y_step(by, (0,)) + z_step(by, (1,))

    def cross(by):
        return z_step(by, (0,)) + y_step(by, (1,))

    w = updated.astype(BF16)
    w_far, theirs = lax.optimization_barrier((send(w, z_step(4)), theirs))
    k0 = jnp.where(low, jnp.stack([w, w_far]), jnp.stack([w_far, w]))
    k_behind, k_ahead = send(k0, turn(1)), send(k0, turn(-1))
    k_top, k_bottom = send(k_behind[0], turn(1)), send(k_ahead[1], turn(-1))
    shape = (2, 2 * chunk, hidden)
    near = jnp.stack([k0, k_behind]).reshape(shape)
    far = jnp.stack([k_ahead, jnp.stack([k_top, k_bottom])]).reshape(shape)
    near_behind, near_ahead = send(near, cross(1)), send(near, cross(-1))
    far_behind, far_ahead = send(far, cross(1)), send(far, cross(-1))
    near_across, far_across = send(near_behind, cross(1)), send(far_ahead, cross(-1))
    own = [near, far, near_behind, far_behind, near_ahead, far_ahead, near_across, far_across]
    crossed = [send(block, core_swap()) for block in own]

    rows_each = inputs.shape[0] // 4
    rows = lax.dynamic_slice_in_dim(inputs, z_low * rows_each, rows_each, 0)
    held = None
    for step in range(4):
        held, last = relay(step, info, rows, held, own, crossed)
        if step < 3:
            rows = send(last, route(lambda x, y, z, core: (x + 1, y, z, core), planes=(step,)))

    def slab(by):
        return lax.dynamic_index_in_dim(held, (z_low + by) % 4, 0, keepdims=False)

    got = [slab(0)] + [
        send(slab(by), route(lambda x, y, z, core, by=by: (x, y, z // 4 * 4 + (z + by) % 4, core)))
        for by in (1, 2, 3)
    ]
    line = jnp.concatenate([got[3], got[2], got[1], got[0], got[3], got[2], got[1]])
    boundary = lax.dynamic_slice_in_dim(line, (3 - z_low) * rows_each, 4 * rows_each, 0)
    wa_next = jnp.where(first, ours, theirs)
    wb_next = jnp.where(first, theirs, ours).T
    return wa_next[None], wb_next[None], boundary[None]


def solution(mesh):
    return jax.shard_map(
        body,
        mesh=mesh,
        in_specs=(
            P("section", "replica", None, None),
            P("section", "replica", None, None),
            P("section", "replica", None),
            P("section", None, "replica"),
            P("section", "replica", None),
            P("section", None, "replica"),
            P("section"),
            P("replica", None),
        ),
        out_specs=(
            P("section", "replica", None),
            P("section", None, "replica"),
            P("section", "replica", None),
        ),
        check_vma=False,
    )
```

```python
import functools

import jax
import jax.numpy as jnp
from jax import lax
from jax.experimental import pallas as pl
from jax.experimental.pallas import tpu as pltpu
from jax.sharding import PartitionSpec as P

AXES = ("section", "replica")
F32, BF16 = jnp.float32, jnp.bfloat16
BOTH = (0, 1)
ORDER = (0, -1, 1, 2)
PLACE = (0, 2, 3, 1)
QUARTERS = (2, 1, 3, 0)


def device(x, y, z, core):
    x, y, z = x % 4, y % 4, z % 8
    return (x * 4 + z % 4) * 16 + y * 4 + (z // 4) * 2 + core


def route(move, cores=BOTH, planes=range(4)):
    return [
        (device(x, y, z, core), device(*move(x, y, z, core)))
        for x in planes
        for y in range(4)
        for z in range(8)
        for core in cores
    ]


def y_step(by, cores=BOTH):
    return route(lambda x, y, z, core: (x, y + by, z, core), cores)


def z_step(by, cores=BOTH):
    return route(lambda x, y, z, core: (x, y, z + by, core), cores)


def core_swap(cores=BOTH):
    return route(lambda x, y, z, core: (x, y, z, 1 - core), cores)


def send(block, pairs):
    return lax.ppermute(block, AXES, pairs)


def pair_kernel(info, a_own, b_own, a_got, b_got, *refs):
    outs, own_v, got_v, own_sem, got_sem = refs[:4], *refs[4:]
    y, core = info[2], info[3]
    quarter = own_v.shape[1]

    def fetch(own, got):
        for at, by in enumerate(QUARTERS):
            rows = pl.ds(pl.multiple_of(lax.rem(y + by, 4) * quarter, 16), quarter)
            pltpu.make_async_copy(own.at[rows], own_v.at[at], own_sem.at[at]).start()
            pltpu.make_async_copy(got.at[rows], got_v.at[at], got_sem.at[at]).start()

    @pl.when(core == 0)
    def _():
        fetch(a_own, a_got)

    @pl.when(core == 1)
    def _():
        fetch(b_own, b_got)

    for at in range(4):
        pltpu.make_async_copy(own_v.at[at], own_v.at[at], own_sem.at[at]).wait()
        pltpu.make_async_copy(got_v.at[at], got_v.at[at], got_sem.at[at]).wait()
        outs[at][...] = (own_v[at].astype(F32) + got_v[at].astype(F32)).astype(BF16)


def pair_sum(info, *blocks):
    height, hidden = blocks[0].shape
    quarter = height // 4
    vmem, hbm = pl.BlockSpec(memory_space=pltpu.VMEM), pl.BlockSpec(memory_space=pltpu.HBM)
    return pl.pallas_call(
        pair_kernel,
        name="pair_sum",
        out_shape=(jax.ShapeDtypeStruct((quarter, hidden), BF16),) * 4,
        in_specs=[pl.BlockSpec(memory_space=pltpu.SMEM)] + [hbm] * 4,
        out_specs=(vmem,) * 4,
        scratch_shapes=[
            pltpu.VMEM((4, quarter, hidden), BF16),
            pltpu.VMEM((4, quarter, hidden), BF16),
            pltpu.SemaphoreType.DMA((4,)),
            pltpu.SemaphoreType.DMA((4,)),
        ],
        compiler_params=pltpu.CompilerParams(vmem_limit_bytes=48 << 20),
    )(info, *[pltpu.with_memory_space_constraint(block, pltpu.HBM) for block in blocks])


def relay_kernel(step, has_held, info, rows_ref, *refs):
    held, refs = (refs[:4], refs[4:]) if has_held else ((), refs)
    own, crossed, outs = refs[:8], refs[8:16], refs[16:20]
    last_ref, wa_v, wb_v, stream, done_v, sem_a, sem_b = refs[20:]
    x, z_low, y, core = info[0], info[1], info[2], info[3]
    hidden = wa_v.shape[2]
    half = hidden // 2
    quarter = own[0].shape[1]

    def load(section):
        place = info[8 + lax.rem(section - z_low + 4, 4)]

        def copy(src, dst_v, side, sem):
            row = lax.rem(y + ORDER[side] + 4, 4) * quarter
            pltpu.make_async_copy(
                src,
                dst_v.at[section, pl.ds(pl.multiple_of(row, 16), quarter)],
                sem.at[section],
            ).start()

        def fetch(a_bufs, b_bufs):
            for message in range(4):

                @pl.when(place == message)
                def _(message=message):
                    for side in range(4):
                        copy(a_bufs[2 * message + side // 2].at[side % 2], wa_v, side, sem_a)

            for part in range(2):

                @pl.when(place // 2 == part)
                def _(part=part):
                    for side in range(4):
                        copy(b_bufs[2 * side + part].at[lax.rem(place, 2)], wb_v, side, sem_b)

        @pl.when(core == 0)
        def _():
            fetch(own, crossed)

        @pl.when(core == 1)
        def _():
            fetch(crossed, own)

    @pl.when(x == step)
    def _():
        load(0)
        stream[...] = rows_ref[...].astype(F32)

        def run(section, carry):
            @pl.when(section < 3)
            def _():
                load(section + 1)

            pltpu.make_async_copy(wa_v.at[section], wa_v.at[section], sem_a.at[section]).wait()
            pltpu.make_async_copy(wb_v.at[section], wb_v.at[section], sem_b.at[section]).wait()

            def layer(step, carry):
                value = stream[...]
                scale = lax.rsqrt(jnp.mean(value * value, axis=-1, keepdims=True) + 1e-5)
                narrow = value.astype(BF16)
                total = None
                for at in range(2):
                    columns = pl.ds(at * half, half)
                    gate = jnp.dot(narrow, wa_v[section, :, columns], preferred_element_type=F32)
                    gate = gate * (0.5 * scale)
                    act = (gate + gate * jnp.tanh(gate)).astype(BF16)
                    part = lax.dot_general(
                        act,
                        wb_v[section, :, columns],
                        (((1,), (1,)), ((), ())),
                        preferred_element_type=F32,
                    )
                    total = part if total is None else total + part
                stream[...] = value + total
                return carry

            lax.fori_loop(0, info[4 + lax.rem(z_low - section + 4, 4)], layer, 0)
            done = stream[...].astype(BF16)
            done_v[section] = done
            stream[...] = done.astype(F32)
            return carry

        lax.fori_loop(0, 4, run, 0)
        last_ref[...] = done_v[3]
        for by in range(4):
            outs[by][...] = done_v[lax.rem(z_low + by, 4)]

    if has_held:

        @pl.when(x != step)
        def _():
            for by in range(4):
                outs[by][...] = held[by][...]


def relay(step, info, rows, held, own, crossed):
    vmem, hbm = pl.BlockSpec(memory_space=pltpu.VMEM), pl.BlockSpec(memory_space=pltpu.HBM)
    count, width = rows.shape
    height, hidden = 4 * own[0].shape[1], own[0].shape[2]
    return pl.pallas_call(
        functools.partial(relay_kernel, step, len(held) > 0),
        name="relay",
        out_shape=(jax.ShapeDtypeStruct((count, width), BF16),) * 5,
        in_specs=[pl.BlockSpec(memory_space=pltpu.SMEM), vmem]
        + [vmem] * len(held)
        + [hbm] * (len(own) + len(crossed)),
        out_specs=(vmem,) * 5,
        scratch_shapes=[
            pltpu.VMEM((4, height, hidden), BF16),
            pltpu.VMEM((4, height, hidden), BF16),
            pltpu.VMEM((count, width), F32),
            pltpu.VMEM((4, count, width), BF16),
            pltpu.SemaphoreType.DMA((4,)),
            pltpu.SemaphoreType.DMA((4,)),
        ],
        compiler_params=pltpu.CompilerParams(vmem_limit_bytes=48 << 20),
    )(info, rows, *held, *own, *crossed)


def line_kernel(info, *refs):
    pieces, out_ref, rows_v = refs[:4], *refs[4:]
    count = pieces[0].shape[0]
    for by, piece in enumerate(pieces):
        start = lax.rem(info[1] - by + 4, 4) * count
        rows_v[pl.ds(pl.multiple_of(start, 16), count), :] = piece[...].astype(F32)
    out_ref[...] = rows_v[...].T.astype(BF16)


def line_up(info, pieces):
    count, width = pieces[0].shape
    vmem = pl.BlockSpec(memory_space=pltpu.VMEM)
    return pl.pallas_call(
        line_kernel,
        name="line_up",
        out_shape=jax.ShapeDtypeStruct((width, 4 * count), BF16),
        in_specs=[pl.BlockSpec(memory_space=pltpu.SMEM)] + [vmem] * 4,
        out_specs=vmem,
        scratch_shapes=[pltpu.VMEM((4 * count, width), F32)],
        compiler_params=pltpu.CompilerParams(vmem_limit_bytes=16 << 20),
    )(info, *pieces)


def body(wa_local, wb_local, wa_master, wb_master, wa_moment, wb_moment, counts, inputs):
    section, replica = lax.axis_index("section"), lax.axis_index("replica")
    x, z_low = section // 4, section % 4
    y, z_high, core = replica // 4, (replica // 2) % 2, replica % 2
    first, low = core == 0, z_high == 0
    replicas = lax.axis_size("replica")
    owned, hidden = wa_master.shape[1], wa_master.shape[2]
    chunk = 2 * owned
    place = jnp.stack([x, z_low, y, core])

    a_own, b_own = wa_local[0, 0], wb_local[0, 0].T
    a_got = send(a_own, core_swap((1,)))
    b_got = send(b_own, core_swap((0,)))
    layers = [counts] + [
        send(counts, route(lambda x, y, z, core, by=by: (x, y, z // 4 * 4 + (z + by) % 4, core)))
        for by in (1, 2, 3)
    ]
    across, ahead, behind, mine = pair_sum(place, a_own, b_own, a_got, b_got)
    gots = send(across, y_step(2)), send(ahead, y_step(1)), send(behind, y_step(-1))
    info = jnp.concatenate([place, *layers, jnp.array(PLACE, jnp.int32)])
    gots, info, wa_master, wb_master, wa_moment, wb_moment = lax.optimization_barrier(
        (gots, info, wa_master, wb_master, wa_moment, wb_moment)
    )
    total = mine.astype(F32) + sum(got.astype(F32) for got in gots)
    top, bottom = total[:chunk], total[chunk:]
    z_got = send(jnp.where(low, bottom, top).astype(BF16), z_step(4))

    gain = 0.7 * 1.9
    a_state = (1.0 - gain) * wa_master[0] - (0.7 * 0.81) * wa_moment[0]
    b_state = ((1.0 - gain) * wb_master[0] - (0.7 * 0.81) * wb_moment[0]).T
    kept = jnp.where(first, a_state, b_state)
    state_got = send(jnp.where(first, b_state, a_state), core_swap())
    state = jnp.concatenate([jnp.where(first, kept, state_got), jnp.where(first, state_got, kept)])
    updated = state + (gain / replicas) * (jnp.where(low, top, bottom) + z_got.astype(F32))
    w = updated.astype(BF16)
    ours = jnp.where(first, updated[:owned], updated[owned:])
    theirs = send(jnp.where(first, updated[owned:], updated[:owned]), core_swap())

    def turn(by):
        return y_step(by, (0,)) + z_step(by, (1,))

    def cross(by):
        return z_step(by, (0,)) + y_step(by, (1,))

    w_far, theirs = lax.optimization_barrier((send(w, z_step(4)), theirs))
    wa_next = jnp.where(first, ours, theirs)[None]
    wb_next = jnp.where(first, theirs, ours).T[None]
    k_low, k_high = jnp.where(low, w, w_far), jnp.where(low, w_far, w)
    k0 = jnp.stack([k_low, k_high])
    k_behind, k_ahead = send(k0, turn(1)), send(k0, turn(-1))
    k_across = jnp.stack([send(k_low, turn(2)), send(k_high, turn(-2))])
    shape = (2, 2 * chunk, hidden)
    near = jnp.stack([k0, k_behind]).reshape(shape)
    far = jnp.stack([k_ahead, k_across]).reshape(shape)
    near_behind, near_ahead = send(near, cross(1)), send(near, cross(-1))
    far_behind, far_ahead = send(far, cross(1)), send(far, cross(-1))
    near_behind, wa_next, wb_next = lax.optimization_barrier((near_behind, wa_next, wb_next))
    near_across, far_across = send(near_behind, cross(1)), send(far_ahead, cross(-1))
    own = [near, far, near_behind, far_behind, near_ahead, far_ahead, near_across, far_across]
    crossed = [send(block, core_swap()) for block in own]

    rows_each = inputs.shape[0] // 4
    rows = lax.dynamic_slice_in_dim(inputs, z_low * rows_each, rows_each, 0)
    held = ()
    for step in range(4):
        *held, last = relay(step, info, rows, held, own, crossed)
        if step < 3:
            rows = send(last, route(lambda x, y, z, core: (x + 1, y, z, core), planes=(step,)))

    pieces = [held[0]] + [
        send(held[by], route(lambda x, y, z, core, by=by: (x, y, z // 4 * 4 + (z + by) % 4, core)))
        for by in (1, 2, 3)
    ]
    boundary = line_up(info, pieces).T
    return wa_next, wb_next, boundary[None]


def solution(mesh):
    return jax.shard_map(
        body,
        mesh=mesh,
        in_specs=(
            P("section", "replica", None, None),
            P("section", "replica", None, None),
            P("section", "replica", None),
            P("section", None, "replica"),
            P("section", "replica", None),
            P("section", None, "replica"),
            P("section"),
            P("replica", None),
        ),
        out_specs=(
            P("section", "replica", None),
            P("section", None, "replica"),
            P("section", "replica", None),
        ),
        check_vma=False,
    )
```

```python
import functools

import jax
import jax.numpy as jnp
from jax import lax
from jax.experimental import pallas as pl
from jax.experimental.layout import Layout, with_layout_constraint
from jax.experimental.pallas import tpu as pltpu
from jax.sharding import PartitionSpec as P

AXES = ("section", "replica")
F32, BF16 = jnp.float32, jnp.bfloat16
BOTH = (0, 1)
ORDER = (0, -1, 1, 2)
PLACE = (0, 2, 3, 1)
QUARTERS = (2, 1, 3, 0)


def device(x, y, z, core):
    x, y, z = x % 4, y % 4, z % 8
    return (x * 4 + z % 4) * 16 + y * 4 + (z // 4) * 2 + core


def route(move, cores=BOTH, planes=range(4)):
    return [
        (device(x, y, z, core), device(*move(x, y, z, core)))
        for x in planes
        for y in range(4)
        for z in range(8)
        for core in cores
    ]


def y_step(by, cores=BOTH):
    return route(lambda x, y, z, core: (x, y + by, z, core), cores)


def z_step(by, cores=BOTH):
    return route(lambda x, y, z, core: (x, y, z + by, core), cores)


def core_swap(cores=BOTH):
    return route(lambda x, y, z, core: (x, y, z, 1 - core), cores)


def send(block, pairs):
    return lax.ppermute(block, AXES, pairs)


def pair_kernel(place, a_own, b_own, a_got, b_got, *refs):
    outs, own_v, got_v, own_sem, got_sem = refs[:8], *refs[8:]
    y, core, z_high = place[0], place[1], place[2]
    chunk = own_v.shape[1]

    def fetch(own, got):
        for at in range(8):
            half = 1 - z_high if at < 4 else z_high
            row = (2 * lax.rem(y + QUARTERS[at % 4], 4) + half) * chunk
            rows = pl.ds(pl.multiple_of(row, 8), chunk)
            pltpu.make_async_copy(own.at[rows], own_v.at[at], own_sem.at[at]).start()
            pltpu.make_async_copy(got.at[rows], got_v.at[at], got_sem.at[at]).start()

    @pl.when(core == 0)
    def _():
        fetch(a_own, a_got)

    @pl.when(core == 1)
    def _():
        fetch(b_own, b_got)

    for at in range(8):
        pltpu.make_async_copy(own_v.at[at], own_v.at[at], own_sem.at[at]).wait()
        pltpu.make_async_copy(got_v.at[at], got_v.at[at], got_sem.at[at]).wait()
        outs[at][...] = (own_v[at].astype(F32) + got_v[at].astype(F32)).astype(BF16)


def pair_sum(place, *blocks):
    height, hidden = blocks[0].shape
    chunk = height // 8
    vmem, hbm = pl.BlockSpec(memory_space=pltpu.VMEM), pl.BlockSpec(memory_space=pltpu.HBM)
    return pl.pallas_call(
        pair_kernel,
        name="pair_sum",
        out_shape=(jax.ShapeDtypeStruct((chunk, hidden), BF16),) * 8,
        in_specs=[pl.BlockSpec(memory_space=pltpu.SMEM)] + [hbm] * 4,
        out_specs=(vmem,) * 8,
        scratch_shapes=[
            pltpu.VMEM((8, chunk, hidden), BF16),
            pltpu.VMEM((8, chunk, hidden), BF16),
            pltpu.SemaphoreType.DMA((8,)),
            pltpu.SemaphoreType.DMA((8,)),
        ],
        compiler_params=pltpu.CompilerParams(vmem_limit_bytes=48 << 20),
    )(place, *[pltpu.with_memory_space_constraint(block, pltpu.HBM) for block in blocks])


def relay_kernel(step, has_held, info, rows_ref, *refs):
    held, refs = (refs[:4], refs[4:]) if has_held else ((), refs)
    own, crossed, outs = refs[:8], refs[8:16], refs[16:20]
    last_ref, wa_v, wb_v, stream, done_v, sem_a, sem_b = refs[20:]
    x, z_low, y, core = info[0], info[1], info[2], info[3]
    hidden = wa_v.shape[2]
    half = hidden // 2
    quarter = own[0].shape[1]

    def load(section):
        place = info[8 + lax.rem(section - z_low + 4, 4)]

        def copy(src, dst_v, side, sem):
            row = lax.rem(y + ORDER[side] + 4, 4) * quarter
            pltpu.make_async_copy(
                src,
                dst_v.at[section, pl.ds(pl.multiple_of(row, 16), quarter)],
                sem.at[section],
            ).start()

        def fetch(a_bufs, b_bufs):
            for message in range(4):

                @pl.when(place == message)
                def _(message=message):
                    for side in range(4):
                        copy(a_bufs[2 * message + side // 2].at[side % 2], wa_v, side, sem_a)

            for part in range(2):

                @pl.when(place // 2 == part)
                def _(part=part):
                    for side in range(4):
                        copy(b_bufs[2 * side + part].at[lax.rem(place, 2)], wb_v, side, sem_b)

        @pl.when(core == 0)
        def _():
            fetch(own, crossed)

        @pl.when(core == 1)
        def _():
            fetch(crossed, own)

    @pl.when(x == step)
    def _():
        load(0)
        stream[...] = rows_ref[...].astype(F32)

        def run(section, carry):
            @pl.when(section < 3)
            def _():
                load(section + 1)

            pltpu.make_async_copy(wa_v.at[section], wa_v.at[section], sem_a.at[section]).wait()
            pltpu.make_async_copy(wb_v.at[section], wb_v.at[section], sem_b.at[section]).wait()

            def layer(step, carry):
                value = stream[...]
                scale = lax.rsqrt(jnp.mean(value * value, axis=-1, keepdims=True) + 1e-5)
                narrow = value.astype(BF16)
                total = None
                for at in range(2):
                    columns = pl.ds(at * half, half)
                    gate = jnp.dot(narrow, wa_v[section, :, columns], preferred_element_type=F32)
                    gate = gate * (0.5 * scale)
                    act = (gate + gate * jnp.tanh(gate)).astype(BF16)
                    part = lax.dot_general(
                        act,
                        wb_v[section, :, columns],
                        (((1,), (1,)), ((), ())),
                        preferred_element_type=F32,
                    )
                    total = part if total is None else total + part
                stream[...] = value + total
                return carry

            lax.fori_loop(0, info[4 + lax.rem(z_low - section + 4, 4)], layer, 0)
            done = stream[...].astype(BF16)
            done_v[section] = done
            stream[...] = done.astype(F32)
            return carry

        lax.fori_loop(0, 4, run, 0)
        last_ref[...] = done_v[3]
        for by in range(4):
            outs[by][...] = done_v[lax.rem(z_low + by, 4)]

    if has_held:

        @pl.when(x != step)
        def _():
            for by in range(4):
                outs[by][...] = held[by][...]


def relay(step, info, rows, held, own, crossed):
    vmem, hbm = pl.BlockSpec(memory_space=pltpu.VMEM), pl.BlockSpec(memory_space=pltpu.HBM)
    count, width = rows.shape
    height, hidden = 4 * own[0].shape[1], own[0].shape[2]
    return pl.pallas_call(
        functools.partial(relay_kernel, step, len(held) > 0),
        name="relay",
        out_shape=(jax.ShapeDtypeStruct((count, width), BF16),) * 5,
        in_specs=[pl.BlockSpec(memory_space=pltpu.SMEM), vmem]
        + [vmem] * len(held)
        + [hbm] * (len(own) + len(crossed)),
        out_specs=(vmem,) * 5,
        scratch_shapes=[
            pltpu.VMEM((4, height, hidden), BF16),
            pltpu.VMEM((4, height, hidden), BF16),
            pltpu.VMEM((count, width), F32),
            pltpu.VMEM((4, count, width), BF16),
            pltpu.SemaphoreType.DMA((4,)),
            pltpu.SemaphoreType.DMA((4,)),
        ],
        compiler_params=pltpu.CompilerParams(vmem_limit_bytes=20 << 20),
    )(info, rows, *held, *own, *crossed)


def line_kernel(info, *refs):
    pieces, out_ref, rows_v = refs[:4], *refs[4:]
    count = pieces[0].shape[0]
    for by, piece in enumerate(pieces):
        start = lax.rem(info[1] - by + 4, 4) * count
        rows_v[pl.ds(pl.multiple_of(start, 16), count), :] = piece[...].astype(F32)
    out_ref[...] = rows_v[...].T.astype(BF16)


def line_up(info, pieces):
    count, width = pieces[0].shape
    vmem = pl.BlockSpec(memory_space=pltpu.VMEM)
    return pl.pallas_call(
        line_kernel,
        name="line_up",
        out_shape=jax.ShapeDtypeStruct((width, 4 * count), BF16),
        in_specs=[pl.BlockSpec(memory_space=pltpu.SMEM)] + [vmem] * 4,
        out_specs=vmem,
        scratch_shapes=[pltpu.VMEM((4 * count, width), F32)],
        compiler_params=pltpu.CompilerParams(vmem_limit_bytes=16 << 20),
    )(info, *pieces)


def body(wa_local, wb_local, wa_master, wb_master, wa_moment, wb_moment, counts, inputs):
    section, replica = lax.axis_index("section"), lax.axis_index("replica")
    x, z_low = section // 4, section % 4
    y, z_high, core = replica // 4, (replica // 2) % 2, replica % 2
    first, low = core == 0, z_high == 0
    replicas = lax.axis_size("replica")
    owned, hidden = wa_master.shape[1], wa_master.shape[2]
    chunk = 2 * owned

    a_own, b_own = wa_local[0, 0], wb_local[0, 0].T
    a_got = send(a_own, core_swap((1,)))
    b_got = send(b_own, core_swap((0,)))
    layers = [counts] + [
        send(counts, route(lambda x, y, z, core, by=by: (x, y, z // 4 * 4 + (z + by) % 4, core)))
        for by in (1, 2, 3)
    ]
    def y_sends(across, ahead, behind):
        return send(across, y_step(2)), send(ahead, y_step(1)), send(behind, y_step(-1))

    *away, away_mine, across, ahead, behind, mine = pair_sum(
        jnp.stack([y, core, z_high]), a_own, b_own, a_got, b_got
    )
    away_gots = y_sends(*away)
    info = jnp.concatenate(
        [jnp.stack([x, z_low, y, core]), *layers, jnp.array(PLACE, jnp.int32)]
    )
    away_gots, kept_parts, info, wa_master, wb_master, wa_moment, wb_moment = (
        lax.optimization_barrier(
            (away_gots, (across, ahead, behind), info, wa_master, wb_master, wa_moment, wb_moment)
        )
    )
    away_total = away_mine.astype(F32) + sum(got.astype(F32) for got in away_gots)
    z_got = send(away_total.astype(BF16), z_step(4))
    total = mine.astype(F32) + sum(got.astype(F32) for got in y_sends(*kept_parts))

    gain = 0.7 * 1.9
    a_state = (1.0 - gain) * wa_master[0] - (0.7 * 0.81) * wa_moment[0]
    b_state = ((1.0 - gain) * wb_master[0] - (0.7 * 0.81) * wb_moment[0]).T
    kept = jnp.where(first, a_state, b_state)
    state_got = send(jnp.where(first, b_state, a_state), core_swap())
    state = jnp.concatenate([jnp.where(first, kept, state_got), jnp.where(first, state_got, kept)])
    updated = state + (gain / replicas) * (total + z_got.astype(F32))
    w = updated.astype(BF16)
    ours = jnp.where(first, updated[:owned], updated[owned:])
    theirs = send(jnp.where(first, updated[owned:], updated[:owned]), core_swap())

    def turn(by):
        return y_step(by, (0,)) + z_step(by, (1,))

    def cross(by):
        return z_step(by, (0,)) + y_step(by, (1,))

    w_far, theirs = lax.optimization_barrier((send(w, z_step(4)), theirs))
    wa_next = with_layout_constraint(
        jnp.where(first, ours, theirs)[None], Layout((1, 0, 2))
    )
    wb_next = with_layout_constraint(
        jnp.where(first, theirs, ours).T[None], Layout((2, 0, 1))
    )
    k_low, k_high = jnp.where(low, w, w_far), jnp.where(low, w_far, w)
    k0 = jnp.stack([k_low, k_high])
    k_behind, k_ahead = send(k0, turn(1)), send(k0, turn(-1))
    k_across = jnp.stack([send(k_low, turn(2)), send(k_high, turn(-2))])
    shape = (2, 2 * chunk, hidden)
    near = jnp.stack([k0, k_behind]).reshape(shape)
    far = jnp.stack([k_ahead, k_across]).reshape(shape)
    rows_each = inputs.shape[0] // 4
    rows = lax.dynamic_slice_in_dim(inputs, z_low * rows_each, rows_each, 0)
    near_behind, far_later, wa_next, wb_next, rows = lax.optimization_barrier(
        (send(near, cross(1)), far, wa_next, wb_next, rows)
    )
    far_ahead, near_later = lax.optimization_barrier((send(far, cross(-1)), near))
    near_across, far_behind = send(near_behind, cross(1)), send(far_later, cross(1))
    far_across, near_ahead = send(far_ahead, cross(-1)), send(near_later, cross(-1))
    own = [near, far, near_behind, far_behind, near_ahead, far_ahead, near_across, far_across]
    crossed = [send(block, core_swap()) for block in own]

    held = ()
    for step in range(4):
        *held, last = relay(step, info, rows, held, own, crossed)
        if step < 3:
            rows = send(last, route(lambda x, y, z, core: (x + 1, y, z, core), planes=(step,)))

    pieces = [held[0]] + [
        send(held[by], route(lambda x, y, z, core, by=by: (x, y, z // 4 * 4 + (z + by) % 4, core)))
        for by in (1, 2, 3)
    ]
    boundary = line_up(info, pieces).T
    return wa_next, wb_next, boundary[None]


def solution(mesh):
    return jax.shard_map(
        body,
        mesh=mesh,
        in_specs=(
            P("section", "replica", None, None),
            P("section", "replica", None, None),
            P("section", "replica", None),
            P("section", None, "replica"),
            P("section", "replica", None),
            P("section", None, "replica"),
            P("section"),
            P("replica", None),
        ),
        out_specs=(
            P("section", "replica", None),
            P("section", None, "replica"),
            P("section", "replica", None),
        ),
        check_vma=False,
    )
```

```python
import functools

import jax
import jax.numpy as jnp
from jax import lax
from jax.experimental import pallas as pl
from jax.experimental.layout import Layout, with_layout_constraint
from jax.experimental.pallas import tpu as pltpu
from jax.sharding import PartitionSpec as P

AXES = ("section", "replica")
F32, BF16 = jnp.float32, jnp.bfloat16
BOTH = (0, 1)
ORDER = (0, -1, 1, 2)
PLACE = (0, 2, 3, 1)
QUARTERS = (2, 1, 3, 0)


def device(x, y, z, core):
    x, y, z = x % 4, y % 4, z % 8
    return (x * 4 + z % 4) * 16 + y * 4 + (z // 4) * 2 + core


def route(move, cores=BOTH, planes=range(4)):
    return [
        (device(x, y, z, core), device(*move(x, y, z, core)))
        for x in planes
        for y in range(4)
        for z in range(8)
        for core in cores
    ]


def y_step(by, cores=BOTH):
    return route(lambda x, y, z, core: (x, y + by, z, core), cores)


def z_step(by, cores=BOTH):
    return route(lambda x, y, z, core: (x, y, z + by, core), cores)


def core_swap(cores=BOTH):
    return route(lambda x, y, z, core: (x, y, z, 1 - core), cores)


def send(block, pairs):
    return lax.ppermute(block, AXES, pairs)


def pair_kernel(place, a_own, b_own, a_got, b_got, *refs):
    outs, own_v, got_v, own_sem, got_sem = refs[:8], *refs[8:]
    y, core, z_high = place[0], place[1], place[2]
    chunk = own_v.shape[1]

    def fetch(own, got):
        for at in range(8):
            half = 1 - z_high if at < 4 else z_high
            row = (2 * lax.rem(y + QUARTERS[at % 4], 4) + half) * chunk
            rows = pl.ds(pl.multiple_of(row, 8), chunk)
            pltpu.make_async_copy(own.at[rows], own_v.at[at], own_sem.at[at]).start()
            pltpu.make_async_copy(got.at[rows], got_v.at[at], got_sem.at[at]).start()

    @pl.when(core == 0)
    def _():
        fetch(a_own, a_got)

    @pl.when(core == 1)
    def _():
        fetch(b_own, b_got)

    for at in range(8):
        pltpu.make_async_copy(own_v.at[at], own_v.at[at], own_sem.at[at]).wait()
        pltpu.make_async_copy(got_v.at[at], got_v.at[at], got_sem.at[at]).wait()
        outs[at][...] = (own_v[at].astype(F32) + got_v[at].astype(F32)).astype(BF16)


def pair_sum(place, *blocks):
    height, hidden = blocks[0].shape
    chunk = height // 8
    vmem, hbm = pl.BlockSpec(memory_space=pltpu.VMEM), pl.BlockSpec(memory_space=pltpu.HBM)
    anywhere = pl.BlockSpec(memory_space=pl.ANY)
    own = [pltpu.with_memory_space_constraint(block, pltpu.HBM) for block in blocks[:2]]
    return pl.pallas_call(
        pair_kernel,
        name="pair_sum",
        out_shape=(jax.ShapeDtypeStruct((chunk, hidden), BF16),) * 8,
        in_specs=[pl.BlockSpec(memory_space=pltpu.SMEM)] + [hbm] * 2 + [anywhere] * 2,
        out_specs=(vmem,) * 8,
        scratch_shapes=[
            pltpu.VMEM((8, chunk, hidden), BF16),
            pltpu.VMEM((8, chunk, hidden), BF16),
            pltpu.SemaphoreType.DMA((8,)),
            pltpu.SemaphoreType.DMA((8,)),
        ],
        compiler_params=pltpu.CompilerParams(vmem_limit_bytes=24 << 20),
    )(place, *own, *blocks[2:])


def pick(index, values):
    value = values[0]
    for at in range(1, len(values)):
        value = jnp.where(index == at, values[at], value)
    return value


def relay_kernel(step, has_held, info, rows_ref, *refs):
    held, refs = (refs[:4], refs[4:]) if has_held else ((), refs)
    own, crossed, outs = refs[:8], refs[8:16], refs[16:20]
    last_ref, wa_v, wb_v, stream, done_v, sem_a, sem_b = refs[20:]
    x, z_low, y, core = info[0], info[1], info[2], info[3]
    hidden = wa_v.shape[2]
    half = hidden // 2
    quarter = own[0].shape[1]

    def load(section):
        place = pick(lax.rem(section - z_low + 4, 4), PLACE)

        def copy(src, dst_v, side, sem):
            row = lax.rem(y + ORDER[side] + 4, 4) * quarter
            pltpu.make_async_copy(
                src,
                dst_v.at[section, pl.ds(pl.multiple_of(row, 16), quarter)],
                sem.at[section],
            ).start()

        def fetch(a_bufs, b_bufs):
            for message in range(4):

                @pl.when(place == message)
                def _(message=message):
                    for side in range(4):
                        copy(a_bufs[2 * message + side // 2].at[side % 2], wa_v, side, sem_a)

            for part in range(2):

                @pl.when(place // 2 == part)
                def _(part=part):
                    for side in range(4):
                        copy(b_bufs[2 * side + part].at[lax.rem(place, 2)], wb_v, side, sem_b)

        @pl.when(core == 0)
        def _():
            fetch(own, crossed)

        @pl.when(core == 1)
        def _():
            fetch(crossed, own)

    @pl.when(x == step)
    def _():
        load(0)
        stream[...] = rows_ref[...].astype(F32)

        def run(section, carry):
            @pl.when(section < 3)
            def _():
                load(section + 1)

            pltpu.make_async_copy(wa_v.at[section], wa_v.at[section], sem_a.at[section]).wait()
            pltpu.make_async_copy(wb_v.at[section], wb_v.at[section], sem_b.at[section]).wait()

            def layer(step, carry):
                value = stream[...]
                scale = lax.rsqrt(jnp.mean(value * value, axis=-1, keepdims=True) + 1e-5)
                narrow = value.astype(BF16)
                total = None
                for at in range(2):
                    columns = pl.ds(at * half, half)
                    gate = jnp.dot(narrow, wa_v[section, :, columns], preferred_element_type=F32)
                    gate = gate * (0.5 * scale)
                    act = (gate + gate * jnp.tanh(gate)).astype(BF16)
                    part = lax.dot_general(
                        act,
                        wb_v[section, :, columns],
                        (((1,), (1,)), ((), ())),
                        preferred_element_type=F32,
                    )
                    total = part if total is None else total + part
                stream[...] = value + total
                return carry

            lax.fori_loop(0, info[4 + lax.rem(z_low - section + 4, 4)], layer, 0)
            done = stream[...].astype(BF16)
            done_v[section] = done
            stream[...] = done.astype(F32)
            return carry

        lax.fori_loop(0, 4, run, 0)
        last_ref[...] = done_v[3]
        for by in range(4):
            outs[by][...] = done_v[lax.rem(z_low + by, 4)]

    if has_held:

        @pl.when(x != step)
        def _():
            for by in range(4):
                outs[by][...] = held[by][...]


def relay(step, info, rows, held, own, crossed):
    blocks = [pltpu.with_memory_space_constraint(block, pltpu.HBM) for block in own + crossed]
    vmem, hbm = pl.BlockSpec(memory_space=pltpu.VMEM), pl.BlockSpec(memory_space=pltpu.HBM)
    count, width = rows.shape
    height, hidden = 4 * own[0].shape[1], own[0].shape[2]
    return pl.pallas_call(
        functools.partial(relay_kernel, step, len(held) > 0),
        name="relay",
        out_shape=(jax.ShapeDtypeStruct((count, width), BF16),) * 5,
        in_specs=[pl.BlockSpec(memory_space=pltpu.SMEM)]
        + [vmem] * (1 + len(held))
        + [hbm] * (len(own) + len(crossed)),
        out_specs=(vmem,) * 5,
        scratch_shapes=[
            pltpu.VMEM((4, height, hidden), BF16),
            pltpu.VMEM((4, height, hidden), BF16),
            pltpu.VMEM((count, width), F32),
            pltpu.VMEM((4, count, width), BF16),
            pltpu.SemaphoreType.DMA((4,)),
            pltpu.SemaphoreType.DMA((4,)),
        ],
        compiler_params=pltpu.CompilerParams(vmem_limit_bytes=24 << 20),
    )(info, rows, *held, *blocks)


def line_kernel(info, *refs):
    pieces, out_ref, rows_v = refs[:4], *refs[4:]
    count = pieces[0].shape[0]
    for by, piece in enumerate(pieces):
        start = lax.rem(info[1] - by + 4, 4) * count
        rows_v[pl.ds(pl.multiple_of(start, 16), count), :] = piece[...].astype(F32)
    out_ref[...] = rows_v[...].T.astype(BF16)


def line_up(info, pieces):
    count, width = pieces[0].shape
    vmem = pl.BlockSpec(memory_space=pltpu.VMEM)
    return pl.pallas_call(
        line_kernel,
        name="line_up",
        out_shape=jax.ShapeDtypeStruct((width, 4 * count), BF16),
        in_specs=[pl.BlockSpec(memory_space=pltpu.SMEM)] + [vmem] * 4,
        out_specs=vmem,
        scratch_shapes=[pltpu.VMEM((4 * count, width), F32)],
        compiler_params=pltpu.CompilerParams(vmem_limit_bytes=16 << 20),
    )(info, *pieces)


def body(wa_local, wb_local, wa_master, wb_master, wa_moment, wb_moment, counts, inputs):
    section, replica = lax.axis_index("section"), lax.axis_index("replica")
    x, z_low = section // 4, section % 4
    y, z_high, core = replica // 4, (replica // 2) % 2, replica % 2
    first, low = core == 0, z_high == 0
    replicas = lax.axis_size("replica")
    owned, hidden = wa_master.shape[1], wa_master.shape[2]
    chunk = 2 * owned

    a_own, b_own = wa_local[0, 0], wb_local[0, 0].T
    a_got = send(a_own, core_swap((1,)))
    b_got = send(b_own, core_swap((0,)))
    gain = 0.7 * 1.9
    a_state = (1.0 - gain) * wa_master[0] - (0.7 * 0.81) * wa_moment[0]
    b_state = ((1.0 - gain) * wb_master[0] - (0.7 * 0.81) * wb_moment[0]).T
    kept = jnp.where(first, a_state, b_state)
    state_got = send(jnp.where(first, b_state, a_state), core_swap())
    state = jnp.concatenate([jnp.where(first, kept, state_got), jnp.where(first, state_got, kept)])
    a_got, b_got, state = lax.optimization_barrier((a_got, b_got, state))
    def y_sends(across, ahead, behind):
        return send(across, y_step(2)), send(ahead, y_step(1)), send(behind, y_step(-1))

    *away, away_mine, across, ahead, behind, mine = pair_sum(
        jnp.stack([y, core, z_high]), a_own, b_own, a_got, b_got
    )
    away_gots = y_sends(*away)
    away_gots, kept_parts = lax.optimization_barrier((away_gots, (across, ahead, behind)))
    away_total = away_mine.astype(F32) + sum(got.astype(F32) for got in away_gots)
    z_got = send(away_total.astype(BF16), z_step(4))
    total = mine.astype(F32) + sum(got.astype(F32) for got in y_sends(*kept_parts))

    updated = state + (gain / replicas) * (total + z_got.astype(F32))
    w = updated.astype(BF16)
    ours = jnp.where(first, updated[:owned], updated[owned:])
    theirs = send(jnp.where(first, updated[owned:], updated[:owned]), core_swap())

    def turn(by):
        return y_step(by, (0,)) + z_step(by, (1,))

    def cross(by):
        return z_step(by, (0,)) + y_step(by, (1,))

    layers = [counts] + [
        send(counts, route(lambda x, y, z, core, by=by: (x, y, z // 4 * 4 + (z + by) % 4, core)))
        for by in (1, 2, 3)
    ]
    w_far, theirs, layers = lax.optimization_barrier((send(w, z_step(4)), theirs, layers))
    wa_next = with_layout_constraint(
        jnp.where(first, ours, theirs)[None], Layout((1, 0, 2))
    )
    wb_next = with_layout_constraint(
        jnp.where(first, theirs, ours).T[None], Layout((2, 0, 1))
    )
    k0 = jnp.where(low, jnp.stack([w, w_far]), jnp.stack([w_far, w]))
    k_behind, k_ahead = send(k0, turn(1)), send(k0, turn(-1))
    k_across = jnp.stack([send(k_behind[0], turn(1)), send(k_ahead[1], turn(-1))])
    shape = (2, 2 * chunk, hidden)
    near = jnp.stack([k0, k_behind]).reshape(shape)
    far = jnp.stack([k_ahead, k_across]).reshape(shape)
    rows_each = inputs.shape[0] // 4
    rows = lax.dynamic_slice_in_dim(inputs, z_low * rows_each, rows_each, 0)
    info = jnp.concatenate([jnp.stack([x, z_low, y, core]), *layers])
    near_behind, far_later, wa_next, wb_next, rows, info = lax.optimization_barrier(
        (send(near, cross(1)), far, wa_next, wb_next, rows, info)
    )
    far_ahead, near_later = lax.optimization_barrier((send(far, cross(-1)), near))
    near_across, far_behind = send(near_behind, cross(1)), send(far_later, cross(1))
    far_across, near_ahead = send(far_ahead, cross(-1)), send(near_later, cross(-1))
    own = [near, far, near_behind, far_behind, near_ahead, far_ahead, near_across, far_across]
    crossed = [send(block, core_swap()) for block in own]

    held = ()
    for step in range(4):
        *held, last = relay(step, info, rows, held, own, crossed)
        if step < 3:
            rows = send(last, route(lambda x, y, z, core: (x + 1, y, z, core), planes=(step,)))

    pieces = [held[0]] + [
        send(held[by], route(lambda x, y, z, core, by=by: (x, y, z // 4 * 4 + (z + by) % 4, core)))
        for by in (1, 2, 3)
    ]
    boundary = line_up(info, pieces).T
    return wa_next, wb_next, boundary[None]


def solution(mesh):
    return jax.shard_map(
        body,
        mesh=mesh,
        in_specs=(
            P("section", "replica", None, None),
            P("section", "replica", None, None),
            P("section", "replica", None),
            P("section", None, "replica"),
            P("section", "replica", None),
            P("section", None, "replica"),
            P("section"),
            P("replica", None),
        ),
        out_specs=(
            P("section", "replica", None),
            P("section", None, "replica"),
            P("section", "replica", None),
        ),
        check_vma=False,
    )
```

```python
import functools

import jax
import jax.numpy as jnp
from jax import lax
from jax.experimental import pallas as pl
from jax.experimental.layout import Layout, with_layout_constraint
from jax.experimental.pallas import tpu as pltpu
from jax.sharding import PartitionSpec as P

AXES = ("section", "replica")
F32, BF16 = jnp.float32, jnp.bfloat16
BOTH = (0, 1)
ORDER = (0, -1, 1, 2)
PLACE = (0, 2, 3, 1)
QUARTERS = (2, 1, 3, 0)


def device(x, y, z, core):
    x, y, z = x % 4, y % 4, z % 8
    return (x * 4 + z % 4) * 16 + y * 4 + (z // 4) * 2 + core


def route(move, cores=BOTH, planes=range(4)):
    return [
        (device(x, y, z, core), device(*move(x, y, z, core)))
        for x in planes
        for y in range(4)
        for z in range(8)
        for core in cores
    ]


def y_step(by, cores=BOTH):
    return route(lambda x, y, z, core: (x, y + by, z, core), cores)


def z_step(by, cores=BOTH):
    return route(lambda x, y, z, core: (x, y, z + by, core), cores)


def core_swap(cores=BOTH):
    return route(lambda x, y, z, core: (x, y, z, 1 - core), cores)


def send(block, pairs):
    return lax.ppermute(block, AXES, pairs)


def pair_kernel(place, a_own, b_own, a_got, b_got, *refs):
    outs, own_v, got_v, own_sem, got_sem = refs[:8], *refs[8:]
    y, core, z_high = place[0], place[1], place[2]
    chunk = own_v.shape[1]

    def fetch(own, got):
        for at in range(8):
            half = 1 - z_high if at < 4 else z_high
            row = (2 * lax.rem(y + QUARTERS[at % 4], 4) + half) * chunk
            rows = pl.ds(pl.multiple_of(row, 8), chunk)
            pltpu.make_async_copy(own.at[rows], own_v.at[at], own_sem.at[at]).start()
            pltpu.make_async_copy(got.at[rows], got_v.at[at], got_sem.at[at]).start()

    @pl.when(core == 0)
    def _():
        fetch(a_own, a_got)

    @pl.when(core == 1)
    def _():
        fetch(b_own, b_got)

    for at in range(8):
        pltpu.make_async_copy(own_v.at[at], own_v.at[at], own_sem.at[at]).wait()
        pltpu.make_async_copy(got_v.at[at], got_v.at[at], got_sem.at[at]).wait()
        outs[at][...] = (own_v[at].astype(F32) + got_v[at].astype(F32)).astype(BF16)


def pair_sum(place, *blocks):
    height, hidden = blocks[0].shape
    chunk = height // 8
    vmem, hbm = pl.BlockSpec(memory_space=pltpu.VMEM), pl.BlockSpec(memory_space=pltpu.HBM)
    anywhere = pl.BlockSpec(memory_space=pl.ANY)
    own = [pltpu.with_memory_space_constraint(block, pltpu.HBM) for block in blocks[:2]]
    return pl.pallas_call(
        pair_kernel,
        name="pair_sum",
        out_shape=(jax.ShapeDtypeStruct((chunk, hidden), BF16),) * 8,
        in_specs=[pl.BlockSpec(memory_space=pltpu.SMEM)] + [hbm] * 2 + [anywhere] * 2,
        out_specs=(vmem,) * 8,
        scratch_shapes=[
            pltpu.VMEM((8, chunk, hidden), BF16),
            pltpu.VMEM((8, chunk, hidden), BF16),
            pltpu.SemaphoreType.DMA((8,)),
            pltpu.SemaphoreType.DMA((8,)),
        ],
        compiler_params=pltpu.CompilerParams(vmem_limit_bytes=24 << 20),
    )(place, *own, *blocks[2:])


def pick(index, values):
    value = values[0]
    for at in range(1, len(values)):
        value = jnp.where(index == at, values[at], value)
    return value


def relay_kernel(step, has_held, info, rows_ref, *refs):
    held, refs = (refs[:4], refs[4:]) if has_held else ((), refs)
    own, crossed, outs = refs[:12], refs[12:24], refs[24:28]
    last_ref, wa_v, wb_v, stream, done_v, sem_a, sem_b = refs[28:]
    x, z_low, y, core = info[0], info[1], info[2], info[3]
    hidden = wa_v.shape[2]
    half = hidden // 2
    quarter = own[0].shape[0]

    def load(section):
        place = pick(lax.rem(section - z_low + 4, 4), PLACE)

        def copy(src, dst_v, side, sem):
            row = lax.rem(y + ORDER[side] + 4, 4) * quarter
            pltpu.make_async_copy(
                src,
                dst_v.at[section, pl.ds(pl.multiple_of(row, 16), quarter)],
                sem.at[section],
            ).start()

        def piece(bufs, message, at):
            here, middle, far = bufs[3 * message : 3 * message + 3]
            return (here, middle.at[0], middle.at[1], far)[at]

        def fetch(a_bufs, b_bufs):
            for at in range(4):

                @pl.when(place == at)
                def _(at=at):
                    for side in range(4):
                        copy(piece(a_bufs, at, side), wa_v, side, sem_a)
                    for side in range(4):
                        copy(piece(b_bufs, side, at), wb_v, side, sem_b)

        @pl.when(core == 0)
        def _():
            fetch(own, crossed)

        @pl.when(core == 1)
        def _():
            fetch(crossed, own)

    @pl.when(x == step)
    def _():
        load(0)
        stream[...] = rows_ref[...].astype(F32)

        def run(section, carry):
            @pl.when(section < 3)
            def _():
                load(section + 1)

            pltpu.make_async_copy(wa_v.at[section], wa_v.at[section], sem_a.at[section]).wait()
            pltpu.make_async_copy(wb_v.at[section], wb_v.at[section], sem_b.at[section]).wait()

            def layer(step, carry):
                value = stream[...]
                scale = lax.rsqrt(jnp.mean(value * value, axis=-1, keepdims=True) + 1e-5)
                narrow = value.astype(BF16)
                total = None
                for at in range(2):
                    columns = pl.ds(at * half, half)
                    gate = jnp.dot(narrow, wa_v[section, :, columns], preferred_element_type=F32)
                    gate = gate * (0.5 * scale)
                    act = (gate + gate * jnp.tanh(gate)).astype(BF16)
                    part = lax.dot_general(
                        act,
                        wb_v[section, :, columns],
                        (((1,), (1,)), ((), ())),
                        preferred_element_type=F32,
                    )
                    total = part if total is None else total + part
                stream[...] = value + total
                return carry

            lax.fori_loop(0, info[4 + lax.rem(z_low - section + 4, 4)], layer, 0)
            done = stream[...].astype(BF16)
            done_v[section] = done
            stream[...] = done.astype(F32)
            return carry

        lax.fori_loop(0, 4, run, 0)
        last_ref[...] = done_v[3]
        for by in range(4):
            outs[by][...] = done_v[lax.rem(z_low + by, 4)]

    if has_held:

        @pl.when(x != step)
        def _():
            for by in range(4):
                outs[by][...] = held[by][...]


def relay(step, info, rows, held, own, crossed):
    blocks = [pltpu.with_memory_space_constraint(block, pltpu.HBM) for block in own + crossed]
    vmem, hbm = pl.BlockSpec(memory_space=pltpu.VMEM), pl.BlockSpec(memory_space=pltpu.HBM)
    count, width = rows.shape
    height, hidden = 4 * own[0].shape[0], own[0].shape[1]
    return pl.pallas_call(
        functools.partial(relay_kernel, step, len(held) > 0),
        name="relay",
        out_shape=(jax.ShapeDtypeStruct((count, width), BF16),) * 5,
        in_specs=[pl.BlockSpec(memory_space=pltpu.SMEM)]
        + [vmem] * (1 + len(held))
        + [hbm] * (len(own) + len(crossed)),
        out_specs=(vmem,) * 5,
        scratch_shapes=[
            pltpu.VMEM((4, height, hidden), BF16),
            pltpu.VMEM((4, height, hidden), BF16),
            pltpu.VMEM((count, width), F32),
            pltpu.VMEM((4, count, width), BF16),
            pltpu.SemaphoreType.DMA((4,)),
            pltpu.SemaphoreType.DMA((4,)),
        ],
        compiler_params=pltpu.CompilerParams(vmem_limit_bytes=24 << 20),
    )(info, rows, *held, *blocks)


def line_kernel(info, *refs):
    pieces, out_ref, rows_v = refs[:4], *refs[4:]
    count = pieces[0].shape[0]
    for by, piece in enumerate(pieces):
        start = lax.rem(info[1] - by + 4, 4) * count
        rows_v[pl.ds(pl.multiple_of(start, 16), count), :] = piece[...].astype(F32)
    out_ref[...] = rows_v[...].T.astype(BF16)


def line_up(info, pieces):
    count, width = pieces[0].shape
    vmem = pl.BlockSpec(memory_space=pltpu.VMEM)
    return pl.pallas_call(
        line_kernel,
        name="line_up",
        out_shape=jax.ShapeDtypeStruct((width, 4 * count), BF16),
        in_specs=[pl.BlockSpec(memory_space=pltpu.SMEM)] + [vmem] * 4,
        out_specs=vmem,
        scratch_shapes=[pltpu.VMEM((4 * count, width), F32)],
        compiler_params=pltpu.CompilerParams(vmem_limit_bytes=16 << 20),
    )(info, *pieces)


def body(wa_local, wb_local, wa_master, wb_master, wa_moment, wb_moment, counts, inputs):
    section, replica = lax.axis_index("section"), lax.axis_index("replica")
    x, z_low = section // 4, section % 4
    y, z_high, core = replica // 4, (replica // 2) % 2, replica % 2
    first, low = core == 0, z_high == 0
    replicas = lax.axis_size("replica")
    owned, hidden = wa_master.shape[1], wa_master.shape[2]
    chunk = 2 * owned

    a_own, b_own = wa_local[0, 0], wb_local[0, 0].T
    a_got = send(a_own, core_swap((1,)))
    b_got = send(b_own, core_swap((0,)))
    gain = 0.7 * 1.9
    a_state = (1.0 - gain) * wa_master[0] - (0.7 * 0.81) * wa_moment[0]
    b_state = ((1.0 - gain) * wb_master[0] - (0.7 * 0.81) * wb_moment[0]).T
    kept = jnp.where(first, a_state, b_state)
    state_got = send(jnp.where(first, b_state, a_state), core_swap())
    state = jnp.concatenate([jnp.where(first, kept, state_got), jnp.where(first, state_got, kept)])
    a_got, b_got, state = lax.optimization_barrier((a_got, b_got, state))
    def y_sends(across, ahead, behind):
        return send(across, y_step(2)), send(ahead, y_step(1)), send(behind, y_step(-1))

    *away, away_mine, across, ahead, behind, mine = pair_sum(
        jnp.stack([y, core, z_high]), a_own, b_own, a_got, b_got
    )
    away_gots = y_sends(*away)
    away_total = away_mine.astype(F32) + sum(got.astype(F32) for got in away_gots)
    away_total, kept_parts = lax.optimization_barrier(
        (away_total.astype(BF16), (across, ahead, behind))
    )
    z_got = send(away_total, z_step(4))
    total = mine.astype(F32) + sum(got.astype(F32) for got in y_sends(*kept_parts))

    updated = state + (gain / replicas) * (total + z_got.astype(F32))
    w = updated.astype(BF16)
    ours = jnp.where(first, updated[:owned], updated[owned:])
    theirs = send(jnp.where(first, updated[owned:], updated[:owned]), core_swap())

    def turn(by):
        return y_step(by, (0,)) + z_step(by, (1,))

    def cross(by):
        return z_step(by, (0,)) + y_step(by, (1,))

    layers = [counts] + [
        send(counts, route(lambda x, y, z, core, by=by: (x, y, z // 4 * 4 + (z + by) % 4, core)))
        for by in (1, 2, 3)
    ]
    w_far, theirs, layers = lax.optimization_barrier((send(w, z_step(4)), theirs, layers))
    wa_next = with_layout_constraint(
        jnp.where(first, ours, theirs)[None], Layout((1, 0, 2))
    )
    wb_next = with_layout_constraint(
        jnp.where(first, theirs, ours).T[None], Layout((2, 0, 1))
    )
    flat = (2 * chunk, hidden)
    k0 = jnp.where(low, jnp.stack([w, w_far]), jnp.stack([w_far, w])).reshape(flat)
    k_behind, k_ahead = send(k0, turn(1)), send(k0, turn(-1))
    k0_behind, k0_ahead = send(k0, cross(1)), send(k0, cross(-1))
    far = jnp.concatenate([send(k_behind[:chunk], turn(1)), send(k_ahead[chunk:], turn(-1))])
    middle = jnp.stack([k_behind, k_ahead])
    info = jnp.concatenate([jnp.stack([x, z_low, y, core]), *layers])
    rows_each = inputs.shape[0] // 4
    rows = lax.dynamic_slice_in_dim(inputs, z_low * rows_each, rows_each, 0)
    middle_behind, middle_ahead = send(middle, cross(1)), send(middle, cross(-1))
    k0_across = send(k0_behind, cross(1))
    far_behind, far_ahead = send(far, cross(1)), send(far, cross(-1))
    early, middle_ahead = lax.optimization_barrier(
        ([k0, middle, far, k0_behind, k0_ahead], middle_ahead)
    )
    k0, middle, far, k0_behind, k0_ahead = early
    middle_across, far_across = send(middle_ahead, cross(-1)), send(far_behind, cross(1))
    far_across, wa_next, wb_next, rows, info = lax.optimization_barrier(
        (far_across, wa_next, wb_next, rows, info)
    )
    own = [k0, middle, far, k0_behind, middle_behind, far_behind]
    own += [k0_ahead, middle_ahead, far_ahead, k0_across, middle_across, far_across]
    crossed = [send(block, core_swap()) for block in own]

    held = ()
    for step in range(4):
        *held, last = relay(step, info, rows, held, own, crossed)
        if step < 3:
            rows = send(last, route(lambda x, y, z, core: (x + 1, y, z, core), planes=(step,)))

    pieces = [held[0]] + [
        send(held[by], route(lambda x, y, z, core, by=by: (x, y, z // 4 * 4 + (z + by) % 4, core)))
        for by in (1, 2, 3)
    ]
    boundary = line_up(info, pieces).T
    return wa_next, wb_next, boundary[None]


def solution(mesh):
    return jax.shard_map(
        body,
        mesh=mesh,
        in_specs=(
            P("section", "replica", None, None),
            P("section", "replica", None, None),
            P("section", "replica", None),
            P("section", None, "replica"),
            P("section", "replica", None),
            P("section", None, "replica"),
            P("section"),
            P("replica", None),
        ),
        out_specs=(
            P("section", "replica", None),
            P("section", None, "replica"),
            P("section", "replica", None),
        ),
        check_vma=False,
    )
```

```python
import functools

import jax
import jax.numpy as jnp
from jax import lax
from jax.experimental import pallas as pl
from jax.experimental.layout import Layout, with_layout_constraint
from jax.experimental.pallas import tpu as pltpu
from jax.sharding import PartitionSpec as P

AXES = ("section", "replica")
F32, BF16 = jnp.float32, jnp.bfloat16
BOTH = (0, 1)
ORDER = (0, -1, 1, 2)
PLACE = (0, 2, 3, 1)
QUARTERS = (2, 1, 3, 0)


def device(x, y, z, core):
    x, y, z = x % 4, y % 4, z % 8
    return (x * 4 + z % 4) * 16 + y * 4 + (z // 4) * 2 + core


def route(move, cores=BOTH, planes=range(4)):
    return [
        (device(x, y, z, core), device(*move(x, y, z, core)))
        for x in planes
        for y in range(4)
        for z in range(8)
        for core in cores
    ]


def y_step(by, cores=BOTH):
    return route(lambda x, y, z, core: (x, y + by, z, core), cores)


def z_step(by, cores=BOTH):
    return route(lambda x, y, z, core: (x, y, z + by, core), cores)


def core_swap(cores=BOTH):
    return route(lambda x, y, z, core: (x, y, z, 1 - core), cores)


def send(block, pairs):
    return lax.ppermute(block, AXES, pairs)


def pair_kernel(place, a_own, b_own, a_got, b_got, *refs):
    outs, own_v, got_v, own_sem, got_sem = refs[:8], *refs[8:]
    y, core, z_high = place[0], place[1], place[2]
    chunk = own_v.shape[1]

    def fetch(own, got):
        for at in range(8):
            half = 1 - z_high if at < 4 else z_high
            row = (2 * lax.rem(y + QUARTERS[at % 4], 4) + half) * chunk
            rows = pl.ds(pl.multiple_of(row, 8), chunk)
            pltpu.make_async_copy(own.at[rows], own_v.at[at], own_sem.at[at]).start()
            pltpu.make_async_copy(got.at[rows], got_v.at[at], got_sem.at[at]).start()

    @pl.when(core == 0)
    def _():
        fetch(a_own, a_got)

    @pl.when(core == 1)
    def _():
        fetch(b_own, b_got)

    for at in range(8):
        pltpu.make_async_copy(own_v.at[at], own_v.at[at], own_sem.at[at]).wait()
        pltpu.make_async_copy(got_v.at[at], got_v.at[at], got_sem.at[at]).wait()
        outs[at][...] = (own_v[at].astype(F32) + got_v[at].astype(F32)).astype(BF16)


def pair_sum(place, *blocks):
    height, hidden = blocks[0].shape
    chunk = height // 8
    vmem, hbm = pl.BlockSpec(memory_space=pltpu.VMEM), pl.BlockSpec(memory_space=pltpu.HBM)
    anywhere = pl.BlockSpec(memory_space=pl.ANY)
    own = [pltpu.with_memory_space_constraint(block, pltpu.HBM) for block in blocks[:2]]
    return pl.pallas_call(
        pair_kernel,
        name="pair_sum",
        out_shape=(jax.ShapeDtypeStruct((chunk, hidden), BF16),) * 8,
        in_specs=[pl.BlockSpec(memory_space=pltpu.SMEM)] + [hbm] * 2 + [anywhere] * 2,
        out_specs=(vmem,) * 8,
        scratch_shapes=[
            pltpu.VMEM((8, chunk, hidden), BF16),
            pltpu.VMEM((8, chunk, hidden), BF16),
            pltpu.SemaphoreType.DMA((8,)),
            pltpu.SemaphoreType.DMA((8,)),
        ],
        compiler_params=pltpu.CompilerParams(vmem_limit_bytes=24 << 20),
    )(place, *own, *blocks[2:])


def pick(index, values):
    value = values[0]
    for at in range(1, len(values)):
        value = jnp.where(index == at, values[at], value)
    return value


def relay_kernel(step, has_held, info, rows_ref, *refs):
    held, refs = (refs[:4], refs[4:]) if has_held else ((), refs)
    own, crossed, outs = refs[:12], refs[12:24], refs[24:28]
    last_ref, wa_v, wb_v, stream, done_v, sem_a, sem_b = refs[28:]
    x, z_low, y, core = info[0], info[1], info[2], info[3]
    hidden = wa_v.shape[2]
    half = hidden // 2
    quarter = own[0].shape[0]

    def load(section):
        place = pick(lax.rem(section - z_low + 4, 4), PLACE)

        def copy(src, dst_v, side, sem):
            row = lax.rem(y + ORDER[side] + 4, 4) * quarter
            pltpu.make_async_copy(
                src,
                dst_v.at[section, pl.ds(pl.multiple_of(row, 16), quarter)],
                sem.at[section],
            ).start()

        def piece(bufs, message, at):
            here, middle, far = bufs[3 * message : 3 * message + 3]
            return (here, middle.at[0], middle.at[1], far)[at]

        def fetch(a_bufs, b_bufs):
            for at in range(4):

                @pl.when(place == at)
                def _(at=at):
                    for side in range(4):
                        copy(piece(a_bufs, at, side), wa_v, side, sem_a)
                    for side in range(4):
                        copy(piece(b_bufs, side, at), wb_v, side, sem_b)

        @pl.when(core == 0)
        def _():
            fetch(own, crossed)

        @pl.when(core == 1)
        def _():
            fetch(crossed, own)

    @pl.when(x == step)
    def _():
        load(0)
        stream[...] = rows_ref[...].astype(F32)

        def run(section, carry):
            @pl.when(section < 3)
            def _():
                load(section + 1)

            pltpu.make_async_copy(wa_v.at[section], wa_v.at[section], sem_a.at[section]).wait()
            pltpu.make_async_copy(wb_v.at[section], wb_v.at[section], sem_b.at[section]).wait()

            def layer(step, carry):
                value = stream[...]
                scale = lax.rsqrt(jnp.mean(value * value, axis=-1, keepdims=True) + 1e-5)
                narrow = value.astype(BF16)
                total = None
                for at in range(2):
                    columns = pl.ds(at * half, half)
                    gate = jnp.dot(narrow, wa_v[section, :, columns], preferred_element_type=F32)
                    gate = gate * (0.5 * scale)
                    act = (gate + gate * jnp.tanh(gate)).astype(BF16)
                    part = lax.dot_general(
                        act,
                        wb_v[section, :, columns],
                        (((1,), (1,)), ((), ())),
                        preferred_element_type=F32,
                    )
                    total = part if total is None else total + part
                stream[...] = value + total
                return carry

            lax.fori_loop(0, info[4 + lax.rem(z_low - section + 4, 4)], layer, 0)
            done = stream[...].astype(BF16)
            done_v[section] = done
            stream[...] = done.astype(F32)
            return carry

        lax.fori_loop(0, 4, run, 0)
        last_ref[...] = done_v[3]
        for by in range(4):
            outs[by][...] = done_v[lax.rem(z_low + by, 4)]

    if has_held:

        @pl.when(x != step)
        def _():
            for by in range(4):
                outs[by][...] = held[by][...]


def relay(step, info, rows, held, own, crossed):
    blocks = [pltpu.with_memory_space_constraint(block, pltpu.HBM) for block in own + crossed]
    vmem, hbm = pl.BlockSpec(memory_space=pltpu.VMEM), pl.BlockSpec(memory_space=pltpu.HBM)
    count, width = rows.shape
    height, hidden = 4 * own[0].shape[0], own[0].shape[1]
    return pl.pallas_call(
        functools.partial(relay_kernel, step, len(held) > 0),
        name="relay",
        out_shape=(jax.ShapeDtypeStruct((count, width), BF16),) * 5,
        in_specs=[pl.BlockSpec(memory_space=pltpu.SMEM)]
        + [vmem] * (1 + len(held))
        + [hbm] * (len(own) + len(crossed)),
        out_specs=(vmem,) * 5,
        scratch_shapes=[
            pltpu.VMEM((4, height, hidden), BF16),
            pltpu.VMEM((4, height, hidden), BF16),
            pltpu.VMEM((count, width), F32),
            pltpu.VMEM((4, count, width), BF16),
            pltpu.SemaphoreType.DMA((4,)),
            pltpu.SemaphoreType.DMA((4,)),
        ],
        compiler_params=pltpu.CompilerParams(vmem_limit_bytes=24 << 20),
    )(info, rows, *held, *blocks)


def line_kernel(info, *refs):
    pieces, out_ref, rows_v = refs[:4], *refs[4:]
    count = pieces[0].shape[0]
    for by, piece in enumerate(pieces):
        start = lax.rem(info[1] - by + 4, 4) * count
        rows_v[pl.ds(pl.multiple_of(start, 16), count), :] = piece[...].astype(F32)
    out_ref[...] = rows_v[...].T.astype(BF16)


def line_up(info, pieces):
    count, width = pieces[0].shape
    vmem = pl.BlockSpec(memory_space=pltpu.VMEM)
    return pl.pallas_call(
        line_kernel,
        name="line_up",
        out_shape=jax.ShapeDtypeStruct((width, 4 * count), BF16),
        in_specs=[pl.BlockSpec(memory_space=pltpu.SMEM)] + [vmem] * 4,
        out_specs=vmem,
        scratch_shapes=[pltpu.VMEM((4 * count, width), F32)],
        compiler_params=pltpu.CompilerParams(vmem_limit_bytes=16 << 20),
    )(info, *pieces)


def body(wa_local, wb_local, wa_master, wb_master, wa_moment, wb_moment, counts, inputs):
    section, replica = lax.axis_index("section"), lax.axis_index("replica")
    x, z_low = section // 4, section % 4
    y, z_high, core = replica // 4, (replica // 2) % 2, replica % 2
    first, low = core == 0, z_high == 0
    replicas = lax.axis_size("replica")
    owned, hidden = wa_master.shape[1], wa_master.shape[2]
    chunk = 2 * owned

    a_own, b_own = wa_local[0, 0], wb_local[0, 0].T
    a_got = send(a_own, core_swap((1,)))
    b_got = send(b_own, core_swap((0,)))
    gain = 0.7 * 1.9
    a_state = (1.0 - gain) * wa_master[0] - (0.7 * 0.81) * wa_moment[0]
    b_state = ((1.0 - gain) * wb_master[0] - (0.7 * 0.81) * wb_moment[0]).T
    kept = jnp.where(first, a_state, b_state)
    state_got = send(jnp.where(first, b_state, a_state), core_swap())
    a_got, b_got, state_got = lax.optimization_barrier((a_got, b_got, state_got))
    state = jnp.concatenate([jnp.where(first, kept, state_got), jnp.where(first, state_got, kept)])
    def y_sends(across, ahead, behind):
        return send(across, y_step(2)), send(ahead, y_step(1)), send(behind, y_step(-1))

    *away, away_mine, across, ahead, behind, mine = pair_sum(
        jnp.stack([y, core, z_high]), a_own, b_own, a_got, b_got
    )
    away_gots = y_sends(*away)
    away_gots, state = lax.optimization_barrier((away_gots, state))
    away_total = away_mine.astype(F32) + sum(got.astype(F32) for got in away_gots)
    away_total, kept_parts = lax.optimization_barrier(
        (away_total.astype(BF16), (across, ahead, behind))
    )
    z_got = send(away_total, z_step(4))
    kept_gots = y_sends(*kept_parts)
    partial = state + (gain / replicas) * (mine.astype(F32) + z_got.astype(F32))
    partial, kept_gots = lax.optimization_barrier((partial, kept_gots))
    updated = partial + (gain / replicas) * sum(got.astype(F32) for got in kept_gots)
    w = updated.astype(BF16)
    ours = jnp.where(first, updated[:owned], updated[owned:])
    theirs = send(jnp.where(first, updated[owned:], updated[:owned]), core_swap())

    def turn(by):
        return y_step(by, (0,)) + z_step(by, (1,))

    def cross(by):
        return z_step(by, (0,)) + y_step(by, (1,))

    layers = [counts] + [
        send(counts, route(lambda x, y, z, core, by=by: (x, y, z // 4 * 4 + (z + by) % 4, core)))
        for by in (1, 2, 3)
    ]
    w_far, theirs, layers = lax.optimization_barrier((send(w, z_step(4)), theirs, layers))
    wa_next = with_layout_constraint(
        jnp.where(first, ours, theirs)[None], Layout((1, 0, 2))
    )
    wb_next = with_layout_constraint(
        jnp.where(first, theirs, ours).T[None], Layout((2, 0, 1))
    )
    flat = (2 * chunk, hidden)
    k0 = jnp.where(low, jnp.stack([w, w_far]), jnp.stack([w_far, w])).reshape(flat)
    k_behind, k_ahead = send(k0, turn(1)), send(k0, turn(-1))
    k0_behind, k0_ahead = send(k0, cross(1)), send(k0, cross(-1))
    far = jnp.concatenate([send(k_behind[:chunk], turn(1)), send(k_ahead[chunk:], turn(-1))])
    middle = jnp.stack([k_behind, k_ahead])
    info = jnp.concatenate([jnp.stack([x, z_low, y, core]), *layers])
    rows_each = inputs.shape[0] // 4
    rows = lax.dynamic_slice_in_dim(inputs, z_low * rows_each, rows_each, 0)
    middle_behind, middle_ahead = send(middle, cross(1)), send(middle, cross(-1))
    k0_across = send(k0_behind, cross(1))
    far_behind, far_ahead = send(far, cross(1)), send(far, cross(-1))
    early, middle_ahead = lax.optimization_barrier(
        ([k0, middle, far, k0_behind, k0_ahead], middle_ahead)
    )
    k0, middle, far, k0_behind, k0_ahead = early
    middle_across, far_across = send(middle_ahead, cross(-1)), send(far_behind, cross(1))
    far_across, wa_next, wb_next, rows, info = lax.optimization_barrier(
        (far_across, wa_next, wb_next, rows, info)
    )
    own = [k0, middle, far, k0_behind, middle_behind, far_behind]
    own += [k0_ahead, middle_ahead, far_ahead, k0_across, middle_across, far_across]
    crossed = [send(block, core_swap()) for block in own]

    held = ()
    for step in range(4):
        *held, last = relay(step, info, rows, held, own, crossed)
        if step < 3:
            rows = send(last, route(lambda x, y, z, core: (x + 1, y, z, core), planes=(step,)))

    pieces = [held[0]] + [
        send(held[by], route(lambda x, y, z, core, by=by: (x, y, z // 4 * 4 + (z + by) % 4, core)))
        for by in (1, 2, 3)
    ]
    boundary = line_up(info, pieces).T
    return wa_next, wb_next, boundary[None]


def solution(mesh):
    return jax.shard_map(
        body,
        mesh=mesh,
        in_specs=(
            P("section", "replica", None, None),
            P("section", "replica", None, None),
            P("section", "replica", None),
            P("section", None, "replica"),
            P("section", "replica", None),
            P("section", None, "replica"),
            P("section"),
            P("replica", None),
        ),
        out_specs=(
            P("section", "replica", None),
            P("section", None, "replica"),
            P("section", "replica", None),
        ),
        check_vma=False,
    )
```

```python
import functools

import jax
import jax.numpy as jnp
from jax import lax
from jax.experimental import pallas as pl
from jax.experimental.layout import Layout, with_layout_constraint
from jax.experimental.pallas import tpu as pltpu
from jax.sharding import PartitionSpec as P

AXES = ("section", "replica")
F32, BF16 = jnp.float32, jnp.bfloat16
BOTH = (0, 1)
ORDER = (0, -1, 1, 2)
PLACE = (0, 2, 3, 1)
QUARTERS = (2, 1, 3, 0)


def device(x, y, z, core):
    x, y, z = x % 4, y % 4, z % 8
    return (x * 4 + z % 4) * 16 + y * 4 + (z // 4) * 2 + core


def route(move, cores=BOTH, planes=range(4)):
    return [
        (device(x, y, z, core), device(*move(x, y, z, core)))
        for x in planes
        for y in range(4)
        for z in range(8)
        for core in cores
    ]


def y_step(by, cores=BOTH):
    return route(lambda x, y, z, core: (x, y + by, z, core), cores)


def z_step(by, cores=BOTH):
    return route(lambda x, y, z, core: (x, y, z + by, core), cores)


def core_swap(cores=BOTH):
    return route(lambda x, y, z, core: (x, y, z, 1 - core), cores)


def send(block, pairs):
    return lax.ppermute(block, AXES, pairs)


def pair_kernel(place, a_own, b_own, a_got, b_got, *refs):
    outs, own_v, got_v, own_sem, got_sem = refs[:8], *refs[8:]
    y, core, z_high = place[0], place[1], place[2]
    chunk = own_v.shape[1]

    def fetch(own, got):
        for at in range(8):
            half = 1 - z_high if at < 4 else z_high
            row = (2 * lax.rem(y + QUARTERS[at % 4], 4) + half) * chunk
            rows = pl.ds(pl.multiple_of(row, 8), chunk)
            pltpu.make_async_copy(own.at[rows], own_v.at[at], own_sem.at[at]).start()
            pltpu.make_async_copy(got.at[rows], got_v.at[at], got_sem.at[at]).start()

    @pl.when(core == 0)
    def _():
        fetch(a_own, a_got)

    @pl.when(core == 1)
    def _():
        fetch(b_own, b_got)

    for at in range(8):
        pltpu.make_async_copy(own_v.at[at], own_v.at[at], own_sem.at[at]).wait()
        pltpu.make_async_copy(got_v.at[at], got_v.at[at], got_sem.at[at]).wait()
        outs[at][...] = own_v[at] + got_v[at]


def pair_sum(place, *blocks):
    height, hidden = blocks[0].shape
    chunk = height // 8
    vmem, hbm = pl.BlockSpec(memory_space=pltpu.VMEM), pl.BlockSpec(memory_space=pltpu.HBM)
    anywhere = pl.BlockSpec(memory_space=pl.ANY)
    own = [pltpu.with_memory_space_constraint(block, pltpu.HBM) for block in blocks[:2]]
    return pl.pallas_call(
        pair_kernel,
        name="pair_sum",
        out_shape=(jax.ShapeDtypeStruct((chunk, hidden), BF16),) * 8,
        in_specs=[pl.BlockSpec(memory_space=pltpu.SMEM)] + [hbm] * 2 + [anywhere] * 2,
        out_specs=(vmem,) * 8,
        scratch_shapes=[
            pltpu.VMEM((8, chunk, hidden), BF16),
            pltpu.VMEM((8, chunk, hidden), BF16),
            pltpu.SemaphoreType.DMA((8,)),
            pltpu.SemaphoreType.DMA((8,)),
        ],
        compiler_params=pltpu.CompilerParams(vmem_limit_bytes=24 << 20),
    )(place, *own, *blocks[2:])


def pick(index, values):
    value = values[0]
    for at in range(1, len(values)):
        value = jnp.where(index == at, values[at], value)
    return value


def relay_kernel(step, has_held, info, rows_ref, *refs):
    held, refs = (refs[:4], refs[4:]) if has_held else ((), refs)
    own, crossed, outs = refs[:12], refs[12:24], refs[24:28]
    last_ref, wa_v, wb_v, stream, done_v, sem_a, sem_b = refs[28:]
    x, z_low, y, core = info[0], info[1], info[2], info[3]
    hidden = wa_v.shape[2]
    half = hidden // 2
    quarter = own[0].shape[0]

    def load(section):
        place = pick(lax.rem(section - z_low + 4, 4), PLACE)

        def copy(src, dst_v, side, sem):
            row = lax.rem(y + ORDER[side] + 4, 4) * quarter
            pltpu.make_async_copy(
                src,
                dst_v.at[section, pl.ds(pl.multiple_of(row, 16), quarter)],
                sem.at[section],
            ).start()

        def piece(bufs, message, at):
            here, middle, far = bufs[3 * message : 3 * message + 3]
            return (here, middle.at[0], middle.at[1], far)[at]

        def fetch(a_bufs, b_bufs):
            for at in range(4):

                @pl.when(place == at)
                def _(at=at):
                    for side in range(4):
                        copy(piece(a_bufs, at, side), wa_v, side, sem_a)
                    for side in range(4):
                        copy(piece(b_bufs, side, at), wb_v, side, sem_b)

        @pl.when(core == 0)
        def _():
            fetch(own, crossed)

        @pl.when(core == 1)
        def _():
            fetch(crossed, own)

    @pl.when(x == step)
    def _():
        load(0)
        stream[...] = rows_ref[...].astype(F32)

        def run(section, carry):
            @pl.when(section < 3)
            def _():
                load(section + 1)

            pltpu.make_async_copy(wa_v.at[section], wa_v.at[section], sem_a.at[section]).wait()
            pltpu.make_async_copy(wb_v.at[section], wb_v.at[section], sem_b.at[section]).wait()

            def layer(step, carry):
                value = stream[...]
                scale = lax.rsqrt(jnp.mean(value * value, axis=-1, keepdims=True) + 1e-5)
                narrow = value.astype(BF16)
                total = None
                for at in range(2):
                    columns = pl.ds(at * half, half)
                    gate = jnp.dot(narrow, wa_v[section, :, columns], preferred_element_type=F32)
                    gate = gate * (0.5 * scale)
                    act = (gate + gate * jnp.tanh(gate)).astype(BF16)
                    part = lax.dot_general(
                        act,
                        wb_v[section, :, columns],
                        (((1,), (1,)), ((), ())),
                        preferred_element_type=F32,
                    )
                    total = part if total is None else total + part
                stream[...] = value + total
                return carry

            lax.fori_loop(0, info[4 + lax.rem(z_low - section + 4, 4)], layer, 0)
            done = stream[...].astype(BF16)
            done_v[section] = done
            stream[...] = done.astype(F32)
            return carry

        lax.fori_loop(0, 4, run, 0)
        last_ref[...] = done_v[3]
        for by in range(4):
            outs[by][...] = done_v[lax.rem(z_low + by, 4)]

    if has_held:

        @pl.when(x != step)
        def _():
            for by in range(4):
                outs[by][...] = held[by][...]


def relay(step, info, rows, held, own, crossed):
    blocks = [pltpu.with_memory_space_constraint(block, pltpu.HBM) for block in own + crossed]
    vmem, hbm = pl.BlockSpec(memory_space=pltpu.VMEM), pl.BlockSpec(memory_space=pltpu.HBM)
    count, width = rows.shape
    height, hidden = 4 * own[0].shape[0], own[0].shape[1]
    return pl.pallas_call(
        functools.partial(relay_kernel, step, len(held) > 0),
        name="relay",
        out_shape=(jax.ShapeDtypeStruct((count, width), BF16),) * 5,
        in_specs=[pl.BlockSpec(memory_space=pltpu.SMEM)]
        + [vmem] * (1 + len(held))
        + [hbm] * (len(own) + len(crossed)),
        out_specs=(vmem,) * 5,
        scratch_shapes=[
            pltpu.VMEM((4, height, hidden), BF16),
            pltpu.VMEM((4, height, hidden), BF16),
            pltpu.VMEM((count, width), F32),
            pltpu.VMEM((4, count, width), BF16),
            pltpu.SemaphoreType.DMA((4,)),
            pltpu.SemaphoreType.DMA((4,)),
        ],
        compiler_params=pltpu.CompilerParams(vmem_limit_bytes=24 << 20),
    )(info, rows, *held, *blocks)


def line_kernel(info, *refs):
    pieces, out_ref, rows_v = refs[:4], *refs[4:]
    count = pieces[0].shape[0]
    for by, piece in enumerate(pieces):
        start = lax.rem(info[1] - by + 4, 4) * count
        rows_v[pl.ds(pl.multiple_of(start, 16), count), :] = piece[...].astype(F32)
    out_ref[...] = rows_v[...].T.astype(BF16)


def line_up(info, pieces):
    count, width = pieces[0].shape
    vmem = pl.BlockSpec(memory_space=pltpu.VMEM)
    return pl.pallas_call(
        line_kernel,
        name="line_up",
        out_shape=jax.ShapeDtypeStruct((width, 4 * count), BF16),
        in_specs=[pl.BlockSpec(memory_space=pltpu.SMEM)] + [vmem] * 4,
        out_specs=vmem,
        scratch_shapes=[pltpu.VMEM((4 * count, width), F32)],
        compiler_params=pltpu.CompilerParams(vmem_limit_bytes=16 << 20),
    )(info, *pieces)


def body(wa_local, wb_local, wa_master, wb_master, wa_moment, wb_moment, counts, inputs):
    section, replica = lax.axis_index("section"), lax.axis_index("replica")
    x, z_low = section // 4, section % 4
    y, z_high, core = replica // 4, (replica // 2) % 2, replica % 2
    first, low = core == 0, z_high == 0
    replicas = lax.axis_size("replica")
    owned, hidden = wa_master.shape[1], wa_master.shape[2]
    chunk = 2 * owned

    a_own, b_own = wa_local[0, 0], wb_local[0, 0].T
    a_got = send(a_own, core_swap((1,)))
    b_got = send(b_own, core_swap((0,)))
    gain = 0.7 * 1.9
    a_state = (1.0 - gain) * wa_master[0] - (0.7 * 0.81) * wa_moment[0]
    b_state = ((1.0 - gain) * wb_master[0] - (0.7 * 0.81) * wb_moment[0]).T
    kept = jnp.where(first, a_state, b_state)
    state_got = send(jnp.where(first, b_state, a_state), core_swap())
    a_got, b_got, state_got = lax.optimization_barrier((a_got, b_got, state_got))
    state = jnp.concatenate([jnp.where(first, kept, state_got), jnp.where(first, state_got, kept)])
    def y_sends(across, ahead, behind):
        return send(across, y_step(2)), send(ahead, y_step(1)), send(behind, y_step(-1))

    *away, away_mine, across, ahead, behind, mine = pair_sum(
        jnp.stack([y, core, z_high]), a_own, b_own, a_got, b_got
    )
    away_gots = y_sends(*away)
    away_gots, state = lax.optimization_barrier((away_gots, state))
    away_total = away_mine.astype(F32) + sum(got.astype(F32) for got in away_gots)
    away_total, kept_parts = lax.optimization_barrier(
        (away_total.astype(BF16), (across, ahead, behind))
    )
    z_got = send(away_total, z_step(4))
    kept_gots = y_sends(*kept_parts)
    partial = state + (gain / replicas) * (mine.astype(F32) + z_got.astype(F32))
    partial, kept_gots = lax.optimization_barrier((partial, kept_gots))
    updated = partial + (gain / replicas) * sum(got.astype(F32) for got in kept_gots)
    w = updated.astype(BF16)
    ours = jnp.where(first, updated[:owned], updated[owned:])
    theirs = send(jnp.where(first, updated[owned:], updated[:owned]), core_swap())

    def turn(by):
        return y_step(by, (0,)) + z_step(by, (1,))

    def cross(by):
        return z_step(by, (0,)) + y_step(by, (1,))

    layers = [counts] + [
        send(counts, route(lambda x, y, z, core, by=by: (x, y, z // 4 * 4 + (z + by) % 4, core)))
        for by in (1, 2, 3)
    ]
    w_far, theirs, layers = lax.optimization_barrier((send(w, z_step(4)), theirs, layers))
    wa_next = with_layout_constraint(
        jnp.where(first, ours, theirs)[None], Layout((1, 0, 2))
    )
    wb_next = with_layout_constraint(
        jnp.where(first, theirs, ours).T[None], Layout((2, 0, 1))
    )
    flat = (2 * chunk, hidden)
    k0 = jnp.where(low, jnp.stack([w, w_far]), jnp.stack([w_far, w])).reshape(flat)
    k_behind, k_ahead = send(k0, turn(1)), send(k0, turn(-1))
    k0_behind, k0_ahead = send(k0, cross(1)), send(k0, cross(-1))
    far = jnp.concatenate([send(k_behind[:chunk], turn(1)), send(k_ahead[chunk:], turn(-1))])
    middle = jnp.stack([k_behind, k_ahead])
    info = jnp.concatenate([jnp.stack([x, z_low, y, core]), *layers])
    rows_each = inputs.shape[0] // 4
    rows = lax.dynamic_slice_in_dim(inputs, z_low * rows_each, rows_each, 0)
    middle_behind, middle_ahead = send(middle, cross(1)), send(middle, cross(-1))
    k0_across = send(k0_behind, cross(1))
    far_behind, far_ahead = send(far, cross(1)), send(far, cross(-1))
    early, middle_ahead = lax.optimization_barrier(
        ([k0, middle, far, k0_behind, k0_ahead], middle_ahead)
    )
    k0, middle, far, k0_behind, k0_ahead = early
    middle_across, far_across = send(middle_ahead, cross(-1)), send(far_behind, cross(1))
    far_across, wa_next, wb_next, rows, info = lax.optimization_barrier(
        (far_across, wa_next, wb_next, rows, info)
    )
    own = [k0, middle, far, k0_behind, middle_behind, far_behind]
    own += [k0_ahead, middle_ahead, far_ahead, k0_across, middle_across, far_across]
    crossed = [send(block, core_swap()) for block in own]

    held = ()
    for step in range(4):
        *held, last = relay(step, info, rows, held, own, crossed)
        if step < 3:
            rows = send(last, route(lambda x, y, z, core: (x + 1, y, z, core), planes=(step,)))

    pieces = [held[0]] + [
        send(held[by], route(lambda x, y, z, core, by=by: (x, y, z // 4 * 4 + (z + by) % 4, core)))
        for by in (1, 2, 3)
    ]
    boundary = line_up(info, pieces).T
    return wa_next, wb_next, boundary[None]


def solution(mesh):
    return jax.shard_map(
        body,
        mesh=mesh,
        in_specs=(
            P("section", "replica", None, None),
            P("section", "replica", None, None),
            P("section", "replica", None),
            P("section", None, "replica"),
            P("section", "replica", None),
            P("section", None, "replica"),
            P("section"),
            P("replica", None),
        ),
        out_specs=(
            P("section", "replica", None),
            P("section", None, "replica"),
            P("section", "replica", None),
        ),
        check_vma=False,
    )
```
